256 devices in a mesh: replica: 64 (over z, y, core), tensor: 4 (over x).
Axes of the slice: x: 4, y: 4, z: 8, core: 2. Of those that a mesh axis runs over, the one named last changes fastest.
Arguments:
- prompt_rows: bfloat16 [8192, 2048], P('replica', 'tensor'), may hold values from -6 to 6
- request_rows: bfloat16 [8192, 2048], P('replica', 'tensor'), may hold values from -6 to 6
- request_keyval_cache: bfloat16 [8192, 64, 512], P('replica', None, 'tensor'), may hold values from -9 to 9
- cache_len: int32 [8192], P('replica'), may hold values from 1 to 64, as said below
- destination: int32 [8192, 1], P('replica'), may hold values from 0 to 63; in each aligned block of 128 rows (0 to 127, 128 to 255, ...) at most 4 rows name the same one
- prefix_cache: bfloat16 [131072, 512], P('replica', 'tensor'), as said below
- attn_gain: float32 [2048], replicated, may hold values from 0.1 to 1.9
- w_query: bfloat16 [2048, 1024], P(None, 'tensor'), may hold values from -0.125 to 0.125
- keyval_weight: bfloat16 [2048, 512], P(None, 'tensor'), may hold values from -0.125 to 0.125
- w_out: bfloat16 [1024, 2048], P('tensor'), may hold values from -0.75 to 0.75
- mlp_gain: float32 [2048], replicated, may hold values from 0.1 to 1.9
- w_gate: bfloat16 [2048, 2560], P(None, 'tensor'), may hold values from -0.125 to 0.125
- w_up: bfloat16 [2048, 2560], P(None, 'tensor'), may hold values from -0.125 to 0.125
- w_down: bfloat16 [2560, 2048], P('tensor'), may hold values from -0.125 to 0.125
Outputs:
- prompt_out: bfloat16 [8192, 2048], P('replica', 'tensor')
- request_out: bfloat16 [8192, 2048], P('replica', 'tensor')
The draws below stay inside these ranges and needn't reach their ends.
Inputs may be any that keep to these rules, and one draw needn't show every extreme that they name: `cache_len`: the first of each replica's 128 requests has exactly 64 cached tokens. `destination`: among the 128 requests of one replica no replica is named more than 4 times, and in every draw some replica is named exactly 4 times by some replica. `prefix_cache`: keys and values of each replica's shared prefix.
All inputs are finite; a program needn't handle non-finite values.
Results may differ from the reference program's by a relative error of at most 0.019.
The reference program's roundings to bfloat16 on the way count: a program that leaves them out, or rounds other values in their place, can miss the bound.
Values may be sent and summed in bfloat16 or wider, within the bound.
A program may use at most 128 MiB of HBM per device.

```python
import math
import jax
import jax.numpy as jnp
import numpy as np
from jax import lax

MODEL_WIDTH = 2048
HQ = 16
KEY_VALUE_HEADS = 4
HEAD_SIZE = 64
FF = 2560
PT = 128
MIG = 128
MAX_CACHED = 64
PFX = 2048
CAP = 4
PROMPTS = 8192
DECODE_REQUESTS = 8192
PREFIX_ROWS = 131072
N_REPLICA = 64
N_TENSOR = 4


def draw_cache_len(key, part):
    lengths = jax.random.randint(key, (DECODE_REQUESTS,), 1, MAX_CACHED + 1)
    leading = jnp.arange(DECODE_REQUESTS) % MIG == 0
    return jnp.where(leading, MAX_CACHED, lengths).astype(jnp.int32)


def draw_prefix_cache(key, part):
    column_list = KEY_VALUE_HEADS * 2 * HEAD_SIZE
    base = jax.random.normal(key, (PREFIX_ROWS, column_list), jnp.float32)
    return base.astype(jnp.bfloat16)


def level_of(key, dims, pieces, least, high):
    factor_of = 1.0
    for dim, blocks in pieces:
        steps = jax.random.uniform(jax.random.fold_in(jax.random.fold_in(key, 6), dim), (blocks,), jnp.float32, least / len(pieces), high / len(pieces))
        factor_of = factor_of * jnp.repeat(jnp.exp(steps), dims[dim] // blocks).reshape((-1,) + (1,) * (len(dims) - 1 - dim))
    return factor_of


def deal_out(rng, own, number, rows, number_of, top, reach, skew):
    sequence = jax.random.permutation(rng, number_of)
    heavy_load, ordinary = portions_of(number_of, rows * top, reach, skew, True), portions_of(number_of, rows * top, reach, skew, False)
    places = jnp.arange(number_of)

    def named(tallies, rotation):
        used = int((tallies > 0).sum())
        fixed = max(1, used // 4)
        shifted = fixed + (places - fixed + rotation * (used - fixed)) % max(1, number_of - fixed)
        return jnp.zeros((number_of,), jnp.int32).at[sequence[jnp.where(places < fixed, places, shifted)]].set(jnp.asarray(tallies, jnp.int32))

    tallies = jnp.where(number % 4 == 0, named(heavy_load, number // 4), named(ordinary, number - number // 4 - 1))
    mixed = jax.random.permutation(jax.random.fold_in(own, 3), number_of)
    giver, taker = mixed[0:number_of // 2 * 2:2], mixed[1:number_of // 2 * 2:2]
    room = jnp.minimum(tallies[giver] - 1, reach - tallies[taker]) // 2
    room = jnp.where((giver == sequence[0]) | (taker == sequence[0]) | (tallies[taker] == 0), 0, jnp.maximum(room, 0))
    shifted = jax.random.randint(jax.random.fold_in(own, 4), (number_of // 2,), 0, 1 << 20) % (room + 1)
    tallies = tallies.at[giver].add(-shifted).at[taker].add(shifted)
    members = jnp.searchsorted(jnp.cumsum(tallies), jnp.arange(rows * top), side="right").astype(jnp.int32)
    listing = members.reshape(top, rows).T
    listing = listing[jax.random.permutation(jax.random.fold_in(own, 1), rows)]
    rotation = jax.random.randint(jax.random.fold_in(own, 2), (rows, 1), 0, top)
    return jnp.take_along_axis(listing, (jnp.arange(top)[None, :] + rotation) % top, axis=1)


def portions_of(amount, total, limit, lean, full):
    portions = [(1 << 20) // math.isqrt(grade ** lean) + 1 for grade in range(1, amount + 1)]
    largest = limit if full else min(limit, max(-(-total // amount), total * portions[0] // sum(portions)))
    least = 1 if total - largest >= amount - 1 else 0
    counts, surplus = [largest] + [least] * (amount - 1), total - largest - least * (amount - 1)
    while surplus > 0:
        candidates = [i for i in range(1, amount) if counts[i] < largest] or [i for i in range(1, amount) if counts[i] < limit]
        pool, remaining = sum([portions[i] for i in candidates]), surplus
        for i in candidates:
            addition = min(limit - counts[i], max(1, remaining * portions[i] // pool), surplus)
            counts[i] = counts[i] + addition
            surplus = surplus - addition
    return np.array(counts)


def centred(own_key, extent, scale, limit, split=(), held_as=jnp.bfloat16):
    entries = scale * jax.random.normal(own_key, extent, jnp.float32)
    if split:
        entries = entries * level_of(own_key, extent, split, -0.22, 0.18)
    return jnp.clip(entries, -limit, limit).astype(held_as)


def setup_inputs(seed: int = 0) -> dict:
    splits = jax.random.split(jax.random.key(seed), 15)
    prompt_rows = centred(splits[0], (PROMPTS, MODEL_WIDTH), 1.0, 6.0, ((0, 64), (1, 4)))
    request_rows = centred(splits[1], (DECODE_REQUESTS, MODEL_WIDTH), 1.0, 6.0, ((0, 64), (1, 4)))
    request_keyval_cache = centred(splits[2], (DECODE_REQUESTS, MAX_CACHED, KEY_VALUE_HEADS * 2 * HEAD_SIZE), 1.5, 9.0, ((0, 64), (2, 4)))
    cache_len = draw_cache_len(jax.random.fold_in(splits[14], 71), 0)
    destination_keys = jax.random.split(jax.random.fold_in(splits[4], 1), DECODE_REQUESTS // MIG)
    destination_turns = jax.random.permutation(jax.random.fold_in(splits[4], 3), DECODE_REQUESTS // MIG)
    destination = jax.vmap(lambda own, number: deal_out(jax.random.fold_in(splits[4], 2), own, number, MIG, N_REPLICA, 1, CAP, 2))(destination_keys, destination_turns).reshape((DECODE_REQUESTS, 1))
    prefix_cache = draw_prefix_cache(jax.random.fold_in(splits[14], 71), 0)
    attn_gain = jnp.clip(1.0 + 0.18 * jax.random.normal(splits[6], (MODEL_WIDTH,), jnp.float32), 0.1, 1.9)
    w_query = centred(splits[7], (MODEL_WIDTH, HQ * HEAD_SIZE), MODEL_WIDTH ** -0.5, 0.125, ((1, 4),))
    keyval_weight = centred(splits[8], (MODEL_WIDTH, KEY_VALUE_HEADS * 2 * HEAD_SIZE), MODEL_WIDTH ** -0.5, 0.125, ((1, 4),))
    w_out = centred(splits[9], (HQ * HEAD_SIZE, MODEL_WIDTH), HEAD_SIZE ** -0.5, 0.75, ((0, 4),))
    mlp_gain = jnp.clip(1.0 + 0.18 * jax.random.normal(splits[10], (MODEL_WIDTH,), jnp.float32), 0.1, 1.9)
    w_gate = centred(splits[11], (MODEL_WIDTH, FF), MODEL_WIDTH ** -0.5, 0.125, ((1, 4),))
    w_up = centred(splits[12], (MODEL_WIDTH, FF), MODEL_WIDTH ** -0.5, 0.125, ((1, 4),))
    w_down = centred(splits[13], (FF, MODEL_WIDTH), FF ** -0.5, 0.125, ((0, 4),))
    return dict(prompt_rows=prompt_rows, request_rows=request_rows, request_keyval_cache=request_keyval_cache, cache_len=cache_len, destination=destination, prefix_cache=prefix_cache, attn_gain=attn_gain, w_query=w_query, keyval_weight=keyval_weight, w_out=w_out, mlp_gain=mlp_gain, w_gate=w_gate, w_up=w_up, w_down=w_down)


EPS = 1e-05

def rms_norm(row_vals, gain_vec):
    values = row_vals.astype(jnp.float32)
    inv_scale = lax.rsqrt(lax.optimization_barrier(jnp.mean(values * values, axis=-1, keepdims=True)) + EPS)
    return (values * inv_scale * gain_vec.astype(jnp.float32)).astype(jnp.bfloat16)

def split_sum(left_rows, right_rows, groups):
    width = left_rows.shape[1] // groups
    summed = jnp.zeros((left_rows.shape[0], right_rows.shape[1]), jnp.float32)
    for group in range(groups):
        product = jnp.dot(left_rows[:, group * width:(group + 1) * width], right_rows[group * width:(group + 1) * width], preferred_element_type=jnp.float32).astype(jnp.bfloat16)
        summed = summed + lax.optimization_barrier(product).astype(jnp.float32)
    return summed

def attend(queries, keyval, visible):
    queries = lax.optimization_barrier(queries)
    keyval = lax.optimization_barrier(keyval)
    row_count = queries.shape[0]
    kv_heads = keyval.shape[1] // (2 * HEAD_SIZE)
    grouped = queries.astype(jnp.float32).reshape(row_count, kv_heads, -1, HEAD_SIZE)
    key_rows = keyval.astype(jnp.float32).reshape(-1, kv_heads, 2, HEAD_SIZE)
    scores = jnp.einsum('rkgd,skd->rkgs', grouped, key_rows[:, :, 0]) * HEAD_SIZE ** (-0.5)
    scores = jnp.where(visible[:, None, None, :], scores, -jnp.inf)
    row_max = lax.optimization_barrier(jnp.max(scores, axis=3, keepdims=True))
    exp_vals = jnp.exp(scores - row_max)
    weights = (exp_vals / lax.optimization_barrier(jnp.sum(exp_vals, axis=3, keepdims=True))).astype(jnp.bfloat16)
    weights = lax.optimization_barrier(weights).astype(jnp.float32)
    mixed_out = jnp.einsum('rkgs,skd->rkgd', weights, key_rows[:, :, 1])
    return mixed_out.reshape(row_count, -1).astype(jnp.bfloat16)

def reference(prompt_rows, request_rows, request_keyval_cache, cache_len, destination, prefix_cache, attn_gain, w_query, keyval_weight, w_out, mlp_gain, w_gate, w_up, w_down):

    def project(row_block):
        normed = rms_norm(row_block, attn_gain)
        queries = jnp.dot(normed, w_query, preferred_element_type=jnp.float32).astype(jnp.bfloat16)
        keyval = jnp.dot(normed, keyval_weight, preferred_element_type=jnp.float32).astype(jnp.bfloat16)
        return (queries, keyval)

    def finish(row_block, attended):
        residual = (row_block.astype(jnp.float32) + split_sum(attended, w_out, N_TENSOR)).astype(jnp.bfloat16)
        normed = rms_norm(residual, mlp_gain)
        gate_act = jnp.dot(normed, w_gate, preferred_element_type=jnp.float32)
        up_act = jnp.dot(normed, w_up, preferred_element_type=jnp.float32)
        hidden = (jax.nn.silu(gate_act) * up_act).astype(jnp.bfloat16)
        return (residual.astype(jnp.float32) + split_sum(hidden, w_down, N_TENSOR)).astype(jnp.bfloat16)
    prefixes = prefix_cache.reshape(N_REPLICA, PFX, -1)
    prompt_q, prompt_kv = project(prompt_rows)
    row_ids = jnp.arange(PT, dtype=jnp.int32)[:, None]
    col_ids = jnp.arange(PFX + PT, dtype=jnp.int32)[None, :]
    prompt_visible = (col_ids < PFX) | (col_ids - PFX <= row_ids)

    def one_prompt(operands):
        query_block, kv_block, prefix_block = operands
        return attend(query_block, jnp.concatenate((prefix_block, kv_block), axis=0), prompt_visible)
    prompt_att = lax.map(one_prompt, (prompt_q.reshape(N_REPLICA, PT, -1), prompt_kv.reshape(N_REPLICA, PT, -1), prefixes))
    prompt_out = finish(prompt_rows, prompt_att.reshape(PROMPTS, -1))
    request_q, request_kv = project(request_rows)
    targets = destination[:, 0].astype(jnp.int32)

    def one_request(operands):
        query_row, kv_row, cache_rows, length, target = operands
        prefix_block = lax.dynamic_index_in_dim(prefixes, target, 0, keepdims=False)
        key_rows = jnp.concatenate((prefix_block, cache_rows, kv_row[None, :]), axis=0)
        visible = jnp.concatenate((jnp.ones((PFX,), bool), jnp.arange(MAX_CACHED, dtype=jnp.int32) < length, jnp.ones((1,), bool)))
        return attend(query_row[None, :], key_rows, visible[None, :])[0]
    request_att = lax.map(one_request, (request_q, request_kv, request_keyval_cache, cache_len.astype(jnp.int32), targets))
    request_out = finish(request_rows, request_att)
    return (prompt_out, request_out)
```

```python
import jax
import jax.numpy as jnp
from jax import lax
from jax.sharding import PartitionSpec as P

HEAD = 64
EPS = 1e-05
BF = jnp.bfloat16
F32 = jnp.float32


def rms_norm(row_vals, gain_vec):
    values = row_vals.astype(F32)
    inv_scale = lax.rsqrt(jnp.mean(values * values, axis=1, keepdims=True) + EPS)
    return (values * inv_scale * gain_vec).astype(BF)


def partial_attend(scores, values, spec="qs,sd->qd"):
    top = jnp.max(scores, axis=-1, keepdims=True)
    weights = jnp.exp(scores - top)
    total = jnp.sum(weights, axis=-1, keepdims=True)
    mixed = jnp.einsum(spec, weights.astype(BF), values, preferred_element_type=F32)
    return mixed, top, total


def merge(parts):
    top = parts[0][1]
    for part in parts[1:]:
        top = jnp.maximum(top, part[1])
    mixed = 0.0
    total = 0.0
    for part in parts:
        factor = jnp.exp(part[1] - top)
        mixed = mixed + part[0] * factor
        total = total + part[2] * factor
    return mixed / total


def body(
    prompt_rows, request_rows, request_keyval_cache, cache_len, destination, prefix_cache,
    attn_gain, w_query, keyval_weight, w_out, mlp_gain, w_gate, w_up, w_down,
):
    replicas = lax.axis_size("replica")
    prompts = prompt_rows.shape[0]
    requests = request_rows.shape[0]
    per_peer = 2 * requests // replicas
    slots = replicas * per_peer
    heads = w_query.shape[1] // HEAD
    scale = HEAD ** -0.5

    rows = jnp.concatenate((prompt_rows, request_rows), axis=0)
    whole = lax.all_gather(rows, "tensor", axis=1, tiled=True)
    normed = rms_norm(whole, attn_gain)
    queries = jnp.dot(normed, w_query, preferred_element_type=F32).astype(BF)
    keyval = jnp.dot(normed, keyval_weight, preferred_element_type=F32).astype(BF)

    target = destination[:, 0]
    earlier = lax.broadcasted_iota(jnp.int32, (requests, requests), 1) < lax.broadcasted_iota(
        jnp.int32, (requests, requests), 0)
    rank = jnp.sum(((target[:, None] == target[None, :]) & earlier).astype(jnp.int32), axis=1)
    place = target * per_peer + rank
    chosen = place[:, None] == lax.broadcasted_iota(jnp.int32, (requests, slots), 1)

    request_q = queries[prompts:]
    sent_q = lax.dot_general(chosen.astype(BF), request_q, (((0,), (0,)), ((), ())),
                             preferred_element_type=F32).astype(BF)
    slot_q = lax.all_to_all(sent_q, "replica", split_axis=0, concat_axis=0, tiled=True)

    keys, values = prefix_cache[:, :HEAD], prefix_cache[:, HEAD:]

    def against_prefix(q):
        flat = q.reshape(-1, HEAD)
        scores = lax.dot_general(flat, keys, (((1,), (1,)), ((), ())), preferred_element_type=F32) * scale
        return partial_attend(scores, values)

    slot_part = against_prefix(slot_q)
    packed = jnp.concatenate(slot_part, axis=1).reshape(slots, -1)
    returned = lax.all_to_all(packed, "replica", split_axis=0, concat_axis=0, tiled=True)
    mine = jnp.take(returned, place, axis=0).reshape(requests * heads, HEAD + 2)

    prompt_q = queries[:prompts]
    prompt_part = against_prefix(prompt_q)
    own = keyval[:prompts]
    flat = prompt_q.reshape(-1, HEAD)
    scores = lax.dot_general(flat, own[:, :HEAD], (((1,), (1,)), ((), ())), preferred_element_type=F32) * scale
    row_ids = lax.broadcasted_iota(jnp.int32, scores.shape, 0) // heads
    col_ids = lax.broadcasted_iota(jnp.int32, scores.shape, 1)
    local_part = partial_attend(jnp.where(col_ids <= row_ids, scores, -jnp.inf), own[:, HEAD:])
    prompt_att = merge((prompt_part, local_part)).reshape(prompts, -1).astype(BF)

    grouped = request_q.reshape(requests, heads, HEAD)
    past = jnp.einsum("shd,sld->shl", grouped, request_keyval_cache[:, :, :HEAD],
                      preferred_element_type=F32) * scale
    alive = lax.broadcasted_iota(jnp.int32, past.shape, 2) < cache_len[:, None, None]
    past_part = partial_attend(
        jnp.where(alive, past, -jnp.inf), request_keyval_cache[:, :, HEAD:], "shl,sld->shd")
    past_part = tuple(v.reshape(requests * heads, -1) for v in past_part)
    own_kv = keyval[prompts:]
    own_score = jnp.sum(grouped.astype(F32) * own_kv[:, None, :HEAD].astype(F32), axis=2, keepdims=True) * scale
    own_val = jnp.broadcast_to(own_kv[:, None, HEAD:].astype(F32), (requests, heads, HEAD)).reshape(-1, HEAD)
    own_part = (own_val, own_score.reshape(-1, 1), jnp.ones((requests * heads, 1), F32))
    far_part = (mine[:, :HEAD], mine[:, HEAD:HEAD + 1], mine[:, HEAD + 1:])
    request_att = merge((far_part, past_part, own_part)).reshape(requests, -1).astype(BF)

    attended = jnp.concatenate((prompt_att, request_att), axis=0)
    head_terms = jnp.dot(attended, w_out, preferred_element_type=F32)
    mixed = lax.psum_scatter(head_terms.astype(BF), "tensor", scatter_dimension=1, tiled=True).astype(F32)
    residual = (rows.astype(F32) + mixed).astype(BF)
    whole_mid = lax.all_gather(residual, "tensor", axis=1, tiled=True)
    normed_mid = rms_norm(whole_mid, mlp_gain)
    gate = jnp.dot(normed_mid, w_gate, preferred_element_type=F32)
    up = jnp.dot(normed_mid, w_up, preferred_element_type=F32)
    hidden = (jax.nn.silu(gate) * up).astype(BF)
    terms = jnp.dot(hidden, w_down, preferred_element_type=F32)
    summed = lax.psum_scatter(terms.astype(BF), "tensor", scatter_dimension=1, tiled=True).astype(F32)
    out = (residual.astype(F32) + summed).astype(BF)
    return out[:prompts], out[prompts:]


def solution(mesh):
    return jax.shard_map(
        body,
        mesh=mesh,
        in_specs=(
            P("replica", "tensor"), P("replica", "tensor"), P("replica", None, "tensor"), P("replica"),
            P("replica", None), P("replica", "tensor"), P(), P(None, "tensor"), P(None, "tensor"),
            P("tensor", None), P(), P(None, "tensor"), P(None, "tensor"), P("tensor", None),
        ),
        out_specs=(P("replica", "tensor"), P("replica", "tensor")),
        check_vma=False,
    )
```

```python
import functools
import math

import jax
import jax.numpy as jnp
from jax import lax
from jax.experimental import pallas as pl
from jax.experimental.pallas import tpu as pltpu
from jax.sharding import PartitionSpec as P

HEAD = 64
EPS = 1e-05
BF = jnp.bfloat16
F32 = jnp.float32
MESH = pl.DeviceIdType.MESH
LOG2E = math.log2(math.e)


def dot(a, b):
    return jnp.dot(a, b, preferred_element_type=F32)


def dot_t(a, b):
    return lax.dot_general(a, b, (((1,), (1,)), ((), ())), preferred_element_type=F32)


def low_lanes(shape):
    return lax.broadcasted_iota(jnp.int32, shape, len(shape) - 1) % 128 < HEAD


def swap(v):
    return pltpu.roll(v, HEAD, 1)


def split_heads(v):
    low = low_lanes(v.shape)
    return jnp.concatenate((jnp.where(low, v, 0.0), jnp.where(low, swap(v), 0.0)), axis=0).astype(BF)


def join_heads(mixed, top):
    n = mixed.shape[0] // 2
    even, odd = mixed[:n], mixed[n:]
    low = low_lanes(even.shape)
    return (
        jnp.where(low, swap(even), odd),
        jnp.where(low, even, swap(odd)),
        jnp.where(low, jnp.broadcast_to(top[:n], even.shape), jnp.broadcast_to(top[n:], even.shape)),
    )


def with_ones(keyval):
    return jnp.where(low_lanes(keyval.shape), jnp.ones_like(keyval), keyval)


def norm(pieces, gain):
    values = jnp.concatenate([p.astype(F32) for p in pieces], axis=1)
    inv_scale = lax.rsqrt(jnp.mean(values * values, axis=1, keepdims=True) + EPS)
    return (values * inv_scale * gain).astype(BF)


def kernel(
    replicas,
    prompt_hbm, request_hbm, cache_hbm, len_hbm, dest_hbm, prefix_hbm, gain_a_hbm, wq_hbm, wkv_hbm, wo_hbm,
    gain_m_hbm, wg_hbm, wu_hbm, wd_hbm,
    prompt_out, request_out,
    dest_v, len_v, gain_a, gain_m, rows_in, mid, prefix, ones_prefix, cache, wq, wkv, wo, wg, wu, wd,
    put, take, q_rows, q_send, q_recv, r_send, r_recv, past, res, terms, far2, from_l, from_r, folded, att,
    lsem, ssem, rsem, xsend, xrecv,
):
    half, width = rows_in.shape[2] // 2, rows_in.shape[3]
    x = lax.axis_index("tensor")
    me = lax.axis_index("replica")
    xr, xl, x2 = lax.rem(x + 1, 4), lax.rem(x + 3, 4), lax.rem(x + 2, 4)
    right, left = {"tensor": xr}, {"tensor": xl}
    scale = HEAD ** -0.5
    base2 = scale * LOG2E
    A, B = pl.ds(0, half), pl.ds(half, half)

    loads = []

    def load(src, dst):
        copy = pltpu.make_async_copy(src, dst, lsem.at[len(loads)])
        copy.start()
        loads.append(copy)
        return copy

    l_dest, l_len = load(dest_hbm, dest_v), load(len_hbm, len_v)
    l_ga, l_gm = load(gain_a_hbm, gain_a), load(gain_m_hbm, gain_m)
    l_req, l_pro = load(request_hbm, rows_in.at[1, x]), load(prompt_hbm, rows_in.at[0, x])
    l_wq, l_wkv = load(wq_hbm, wq), load(wkv_hbm, wkv)
    l_prefix, l_cache = load(prefix_hbm, prefix), load(cache_hbm, cache)
    l_wo = [load(wo_hbm.at[:, pl.ds(d * width, width)], wo.at[d]) for d in range(4)]
    l_wg, l_wu = load(wg_hbm, wg), load(wu_hbm, wu)
    l_wd = [load(wd_hbm.at[:, pl.ds(d * width, width)], wd.at[d]) for d in range(4)]

    barrier = pltpu.get_barrier_semaphore()
    pl.semaphore_signal(barrier, inc=1, device_id=right, device_id_type=MESH)
    pl.semaphore_signal(barrier, inc=1, device_id=left, device_id_type=MESH)

    def greet(k, c):
        pl.semaphore_signal(barrier, inc=1, device_id={"replica": lax.rem(me + k, replicas)}, device_id_type=MESH)
        return c

    lax.fori_loop(1, replicas, greet, 0)
    pl.semaphore_wait(barrier, replicas + 1)

    sent = []

    def ring(base, i, src, dst, to):
        copy = pltpu.make_async_remote_copy(
            src_ref=src, dst_ref=dst, send_sem=ssem.at[base + i], recv_sem=rsem.at[base + i],
            device_id=to, device_id_type=MESH)
        sent.append(copy)
        return copy

    def gather(base, own, whole):
        own_a, own_b = own
        return [
            ring(base, 0, own_a, whole.at[x, A], right), ring(base, 1, own_b, whole.at[x, B], left),
            ring(base, 2, own_b, whole.at[x, B], right), ring(base, 3, own_a, whole.at[x, A], left),
            ring(base, 4, whole.at[xl, A], whole.at[xl, A], right), ring(base, 5, whole.at[xr, B], whole.at[xr, B], left),
        ]

    def begin(msgs):
        for m in msgs[:4]:
            m.start()

    def forward(msgs):
        for i in range(2):
            msgs[i].wait_recv()
            msgs[4 + i].start()

    def arrived(msgs):
        for m in msgs[2:]:
            m.wait_recv()

    def scatter(base, s):
        t = terms.at[s]
        return [
            ring(base, 0, t.at[x2, A], far2.at[s, 0], right), ring(base, 1, t.at[x2, B], far2.at[s, 1], left),
            ring(base, 2, t.at[xr, B], from_l.at[s, B], right), ring(base, 3, t.at[xl, A], from_r.at[s, A], left),
            ring(base, 4, folded.at[s, 0], from_l.at[s, A], right), ring(base, 5, folded.at[s, 1], from_r.at[s, B], left),
        ]

    def spread(msgs, s, make):
        terms[s, x2] = make(x2).astype(BF)
        msgs[0].start()
        msgs[1].start()
        terms[s, xr] = make(xr).astype(BF)
        msgs[2].start()
        terms[s, xl] = make(xl).astype(BF)
        msgs[3].start()
        terms[s, x] = make(x).astype(BF)

    def fold(msgs, s):
        for i, part in enumerate(((xr, A), (xl, B))):
            msgs[i].wait_recv()
            folded[s, i] = (terms[s, part[0], part[1]].astype(F32) + far2[s, i].astype(F32)).astype(BF)
            msgs[4 + i].start()

    def summed(msgs, s):
        for m in msgs[2:]:
            m.wait_recv()
        return terms[s, x].astype(F32) + (from_l[s].astype(F32) + from_r[s].astype(F32))

    g_req = gather(0, (request_hbm.at[A], request_hbm.at[B]), rows_in.at[1])
    g_pro = gather(6, (prompt_hbm.at[A], prompt_hbm.at[B]), rows_in.at[0])
    begin(g_req)

    n = dest_v.shape[0]
    l_dest.wait()
    eye = lax.broadcasted_iota(jnp.int32, (n, n), 0) - lax.broadcasted_iota(jnp.int32, (n, n), 1)
    dest_col = dest_v[...].astype(F32)
    dest_mat = jnp.broadcast_to(dest_col, (n, n))
    dest_row = jnp.sum(jnp.where(eye == 0, dest_mat, 0.0), axis=0, keepdims=True)
    same = dest_mat == jnp.broadcast_to(dest_row, (n, n))
    rank_col = jnp.sum(jnp.where(same & (eye > 0), 1.0, 0.0), axis=1, keepdims=True)
    rank_row = jnp.sum(jnp.where(same & (eye < 0), 1.0, 0.0), axis=0, keepdims=True)
    me_f = me.astype(F32)

    def block_of(dest):
        gap = dest - me_f
        return jnp.where(gap < 0, gap + replicas, gap)

    put_row = block_of(dest_row) * 8 + rank_row
    put_row = jnp.concatenate((put_row, put_row + 4), axis=1)
    slots = replicas * 8
    put[...] = jnp.where(
        jnp.broadcast_to(put_row, (slots, 2 * n)) == lax.broadcasted_iota(jnp.int32, (slots, 2 * n), 0).astype(F32),
        1.0, 0.0).astype(BF)
    take_col = block_of(dest_col) * 16 + rank_col
    take_col = jnp.concatenate((take_col, take_col + 4, take_col + 8, take_col + 12), axis=0)
    take[...] = jnp.where(
        jnp.broadcast_to(take_col, (4 * n, 2 * slots))
        == lax.broadcasted_iota(jnp.int32, (4 * n, 2 * slots), 1).astype(F32), 1.0, 0.0).astype(BF)

    l_prefix.wait()
    ones_prefix[...] = with_ones(prefix[...])
    l_len.wait()
    len_mat = jnp.broadcast_to(len_v[...].astype(F32), (n, n))
    len_col = jnp.sum(jnp.where(eye == 0, len_mat, 0.0), axis=1, keepdims=True)

    forward(g_req)
    begin(g_pro)
    l_ga.wait()
    l_wq.wait()
    l_wkv.wait()
    l_req.wait()
    arrived(g_req)

    def project(s):
        normed = norm([rows_in[s, d] for d in range(4)], gain_a[...])
        return dot(normed, wq[...]).astype(BF), dot(normed, wkv[...]).astype(BF)

    q_req, kv_req = project(1)
    stacked = jnp.concatenate((q_req[:, :128], q_req[:, 128:]), axis=0)
    q_rows[0] = stacked[:n].astype(F32)
    q_rows[1] = stacked[n:].astype(F32)
    q_send[...] = dot(put[...], stacked).reshape(replicas, 8, 128).astype(BF)

    batches = 4
    per = replicas // batches

    def travel(buf_out, buf_in, k, sem, sign):
        return pltpu.make_async_remote_copy(
            src_ref=buf_out.at[k], dst_ref=buf_in.at[k], send_sem=xsend.at[sem], recv_sem=xrecv.at[sem],
            device_id={"replica": lax.rem(me + replicas + sign * k, replicas)}, device_id_type=MESH)

    def launch(buf_out, buf_in, b, sem, sign):
        def one(k, c):
            travel(buf_out, buf_in, k, sem, sign).start()
            return c
        lax.fori_loop(max(1, b * per), (b + 1) * per, one, 0)

    def whole_batch(buf_out, buf_in, b, sem):
        first = max(1, b * per)
        part = pl.ds(first, (b + 1) * per - first)
        return pltpu.make_async_remote_copy(
            src_ref=buf_out.at[part], dst_ref=buf_in.at[part], send_sem=xsend.at[sem], recv_sem=xrecv.at[sem],
            device_id={"replica": lax.rem(me + 1, replicas)}, device_id_type=MESH)

    for b in range(batches):
        launch(q_send, q_recv, b, b, 1)
    q_recv[0] = q_send[0]
    forward(g_pro)

    l_cache.wait()
    group = 8
    cols = group * cache.shape[1]
    row_id = lax.broadcasted_iota(jnp.int32, (group, cols), 0)
    col_id = lax.broadcasted_iota(jnp.int32, (group, cols), 1)
    position = (col_id - row_id * cache.shape[1]).astype(F32)
    for g in range(n // group):
        part = slice(g * group, (g + 1) * group)
        q4 = jnp.concatenate([split_heads(q_rows[hp, part]) for hp in range(2)], axis=0)
        keys = cache[part].reshape(cols, 128)
        alive = (position >= 0) & (position < jnp.broadcast_to(len_col[part], (group, cols)))
        alive = jnp.concatenate((alive,) * 4, axis=0)
        scores = jnp.where(alive, dot_t(q4, keys), -jnp.inf)
        top = jnp.max(scores, axis=1, keepdims=True)
        weights = jnp.exp2(scores * base2 - top * base2).astype(BF)
        mixed = dot(weights, with_ones(keys))
        for hp in range(2):
            joined = join_heads(mixed[hp * 2 * group:(hp + 1) * 2 * group], top[hp * 2 * group:(hp + 1) * 2 * group])
            for i in range(3):
                past[i, hp, part] = joined[i]

    def attend(q, local=None):
        scores = dot_t(q, prefix[...])
        top = jnp.max(scores, axis=1, keepdims=True)
        if local is not None:
            near = dot_t(q, local)
            m = near.shape[1]
            seen = (lax.broadcasted_iota(jnp.int32, near.shape, 1)
                    <= lax.rem(lax.broadcasted_iota(jnp.int32, near.shape, 0), m))
            near = jnp.where(seen, near, -jnp.inf)
            top = jnp.maximum(top, jnp.max(near, axis=1, keepdims=True))
        shift = top * base2
        mixed = dot(jnp.exp2(scores * base2 - shift).astype(BF), ones_prefix[...])
        if local is not None:
            mixed = mixed + dot(jnp.exp2(near * base2 - shift).astype(BF), with_ones(local))
        return join_heads(mixed, top)

    l_pro.wait()
    arrived(g_pro)
    q_pro, kv_pro = project(0)
    for hp in range(2):
        above, total, _ = attend(split_heads(q_pro[:, hp * 128:(hp + 1) * 128].astype(F32)), kv_pro)
        att[0, :, hp * 128:(hp + 1) * 128] = (above / total).astype(BF)

    for c in l_wo:
        c.wait()
    s_pro = scatter(12, 0)
    spread(s_pro, 0, lambda d: dot(att[0], wo[d]))

    lane = lax.rem(lax.broadcasted_iota(jnp.int32, (per * 8, 128), 1), HEAD)

    def serve(b):
        whole_batch(q_send, q_recv, b, b).wait_recv()
        rows = q_recv[b * per:(b + 1) * per].astype(F32).reshape(per * 8, 128)
        above, total, top = attend(split_heads(rows))
        level = top * scale + jnp.log(total)
        hi = level.astype(BF).astype(F32)
        mid_part = (level - hi).astype(BF).astype(F32)
        lo = level - hi - mid_part
        stat = jnp.where(lane < 16, hi, jnp.where(lane < 32, mid_part, lo))
        packed = jnp.concatenate(
            ((above / total).reshape(per, 8, 128), stat.reshape(per, 8, 128)), axis=1)
        r_send[b * per:(b + 1) * per] = packed.astype(BF)
        launch(r_send, r_recv, b, batches + b, -1)

    def settle(msgs, s):
        row = rows_in[s, x].astype(F32)
        mid[s, x] = (row + summed(msgs, s)).astype(BF)
        return None

    def feed(base, s):
        own = mid.at[s, x]
        return gather(base, (own.at[A], own.at[B]), mid.at[s])

    def hidden_of(s):
        normed = norm([mid[s, d] for d in range(4)], gain_m[...])
        gate = dot(normed, wg[...])
        up = dot(normed, wu[...])
        return (gate / (1.0 + jnp.exp(-gate)) * up).astype(BF)

    serve(0)
    fold(s_pro, 0)
    r_recv[0] = r_send[0]
    serve(1)
    settle(s_pro, 0)
    m_pro = feed(18, 0)
    begin(m_pro)
    serve(2)
    forward(m_pro)
    serve(3)
    arrived(m_pro)
    l_gm.wait()
    l_wg.wait()
    l_wu.wait()
    for c in l_wd:
        c.wait()
    hid = hidden_of(0)
    d_pro = scatter(24, 2)
    spread(d_pro, 2, lambda d: dot(hid, wd[d]))

    for b in range(batches):
        whole_batch(r_send, r_recv, b, batches + b).wait_recv()
    back = dot(take[...], r_recv[...].reshape(2 * slots, 128))
    far_mix = back[:2 * n]
    e_row = lax.broadcasted_iota(jnp.int32, (128, 128), 0)
    e_col = lax.broadcasted_iota(jnp.int32, (128, 128), 1)
    pick = ((e_row < HEAD) == (e_col < HEAD)) & (
        (lax.rem(e_row, HEAD) == 0) | (lax.rem(e_row, HEAD) == 16) | (lax.rem(e_row, HEAD) == 32))
    far_level = dot(back[2 * n:].astype(BF), jnp.where(pick, 1.0, 0.0).astype(BF))
    q2 = q_rows[...].reshape(2 * n, 128)
    kv = kv_req.astype(F32)
    low = low_lanes(kv.shape)
    key2 = jnp.where(low, kv, swap(kv))
    val2 = jnp.where(low, swap(kv), kv)
    key2 = jnp.concatenate((key2, key2), axis=0)
    val2 = jnp.concatenate((val2, val2), axis=0)
    prod = q2 * key2
    low2 = low_lanes(prod.shape)
    own_even = jnp.sum(jnp.where(low2, prod, 0.0), axis=1, keepdims=True)
    own_odd = jnp.sum(jnp.where(low2, 0.0, prod), axis=1, keepdims=True)
    own = jnp.where(low2, jnp.broadcast_to(own_even, prod.shape), jnp.broadcast_to(own_odd, prod.shape)) * scale
    p_mix, p_total, p_top = past[0].reshape(2 * n, 128), past[1].reshape(2 * n, 128), past[2].reshape(2 * n, 128) * scale
    top = jnp.maximum(jnp.maximum(far_level, p_top), own)
    w_far, w_past, w_own = jnp.exp(far_level - top), jnp.exp(p_top - top), jnp.exp(own - top)
    merged = (far_mix * w_far + p_mix * w_past + val2 * w_own) / (w_far + p_total * w_past + w_own)
    att[1] = jnp.concatenate((merged[:n], merged[n:]), axis=1).astype(BF)

    s_req = scatter(30, 1)
    spread(s_req, 1, lambda d: dot(att[1], wo[d]))
    fold(d_pro, 2)
    fold(s_req, 1)
    prompt_out[...] = (mid[0, x].astype(F32) + summed(d_pro, 2)).astype(BF)
    settle(s_req, 1)
    m_req = feed(36, 1)
    begin(m_req)
    forward(m_req)
    arrived(m_req)
    hid_r = hidden_of(1)
    d_req = scatter(42, 3)
    spread(d_req, 3, lambda d: dot(hid_r, wd[d]))
    fold(d_req, 3)
    request_out[...] = (mid[1, x].astype(F32) + summed(d_req, 3)).astype(BF)

    for c in sent:
        c.wait_send()
    for b in range(batches):
        whole_batch(q_send, q_recv, b, b).wait_send()
        whole_batch(r_send, r_recv, b, batches + b).wait_send()


def body(
    prompt_rows, request_rows, request_keyval_cache, cache_len, destination, prefix_cache,
    attn_gain, w_query, keyval_weight, w_out, mlp_gain, w_gate, w_up, w_down,
):
    replicas = lax.axis_size("replica")
    n, width = request_rows.shape
    model = w_query.shape[0]
    units = w_gate.shape[1]
    cached = request_keyval_cache.shape[1]
    pre = prefix_cache.shape[0]
    V = pltpu.VMEM
    DMA = pltpu.SemaphoreType.DMA
    out = jax.ShapeDtypeStruct((n, width), BF)
    anyspec = pl.BlockSpec(memory_space=pl.ANY)
    vspec = pl.BlockSpec(memory_space=pltpu.VMEM)
    half = n // 2
    return pl.pallas_call(
        functools.partial(kernel, replicas),
        out_shape=(out, out),
        in_specs=[anyspec] * 14,
        out_specs=(vspec, vspec),
        scratch_shapes=[
            V((n, 1), jnp.int32), V((1, n), jnp.int32), V((1, model), F32), V((1, model), F32),
            V((2, 4, n, width), BF), V((2, 4, n, width), BF),
            V((pre, 128), BF), V((pre, 128), BF), V((n, cached, 128), BF),
            V((model, 256), BF), V((model, 128), BF), V((4, 256, width), BF),
            V((model, units), BF), V((model, units), BF), V((4, units, width), BF),
            V((replicas * 8, 2 * n), BF), V((4 * n, replicas * 16), BF), V((2, n, 128), F32),
            V((replicas, 8, 128), BF), V((replicas, 8, 128), BF),
            V((replicas, 16, 128), BF), V((replicas, 16, 128), BF),
            V((3, 2, n, 128), F32), V((8, 128), BF),
            V((4, 4, n, width), BF), V((4, 2, half, width), BF),
            V((4, n, width), BF), V((4, n, width), BF), V((4, 2, half, width), BF), V((2, n, 256), BF),
            DMA((20,)), DMA((48,)), DMA((48,)), DMA((8,)), DMA((8,)),
        ],
        compiler_params=pltpu.CompilerParams(
            collective_id=0, has_side_effects=True, vmem_limit_bytes=60 * 1024 * 1024),
    )(
        prompt_rows, request_rows, request_keyval_cache, cache_len.reshape(1, n), destination, prefix_cache,
        attn_gain.reshape(1, model), w_query, keyval_weight, w_out, mlp_gain.reshape(1, model), w_gate, w_up, w_down,
    )


def solution(mesh):
    return jax.shard_map(
        body,
        mesh=mesh,
        in_specs=(
            P("replica", "tensor"), P("replica", "tensor"), P("replica", None, "tensor"), P("replica"),
            P("replica", None), P("replica", "tensor"), P(), P(None, "tensor"), P(None, "tensor"),
            P("tensor", None), P(), P(None, "tensor"), P(None, "tensor"), P("tensor", None),
        ),
        out_specs=(P("replica", "tensor"), P("replica", "tensor")),
        check_vma=False,
    )
```

```python
import functools
import math

import jax
import jax.numpy as jnp
from jax import lax
from jax.experimental import pallas as pl
from jax.experimental.pallas import tpu as pltpu
from jax.sharding import PartitionSpec as P

HEAD = 64
EPS = 1e-05
BF = jnp.bfloat16
F32 = jnp.float32
MESH = pl.DeviceIdType.MESH
LOG2E = math.log2(math.e)


def dot(a, b):
    return jnp.dot(a, b, preferred_element_type=F32)


def dot_t(a, b):
    return lax.dot_general(a, b, (((1,), (1,)), ((), ())), preferred_element_type=F32)


def low_lanes(shape):
    return lax.broadcasted_iota(jnp.int32, shape, len(shape) - 1) % 128 < HEAD


def swap(v):
    return pltpu.roll(v, HEAD, 1)


def split_heads(v):
    low = low_lanes(v.shape)
    return jnp.concatenate((jnp.where(low, v, 0.0), jnp.where(low, swap(v), 0.0)), axis=0).astype(BF)


def join_heads(mixed, top):
    n = mixed.shape[0] // 2
    even, odd = mixed[:n], mixed[n:]
    low = low_lanes(even.shape)
    return (
        jnp.where(low, swap(even), odd),
        jnp.where(low, even, swap(odd)),
        jnp.where(low, jnp.broadcast_to(top[:n], even.shape), jnp.broadcast_to(top[n:], even.shape)),
    )


def with_ones(keyval):
    return jnp.where(low_lanes(keyval.shape), jnp.ones_like(keyval), keyval)


def norm(pieces, gain):
    values = jnp.concatenate([p.astype(F32) for p in pieces], axis=1)
    inv_scale = lax.rsqrt(jnp.mean(values * values, axis=1, keepdims=True) + EPS)
    return (values * inv_scale * gain).astype(BF)


def kernel(
    replicas,
    prompt_hbm, request_hbm, cache_hbm, len_hbm, dest_hbm, prefix_hbm, gain_a_hbm, wq_hbm, wkv_hbm, wo_hbm,
    gain_m_hbm, wg_hbm, wu_hbm, wd_hbm,
    prompt_out, request_out,
    dest_v, len_v, gain_a, gain_m, rows_in, mid, prefix, ones_prefix, cache, wq, wkv, wo, wg, wu, wd,
    put, take, q_rows, q_send, q_recv, r_send, r_recv, past, res, terms, far2, from_l, from_r, folded, att,
    lsem, ssem, rsem, xsend, xrecv,
):
    half, width = rows_in.shape[2] // 2, rows_in.shape[3]
    x = lax.axis_index("tensor")
    me = lax.axis_index("replica")
    xr, xl, x2 = lax.rem(x + 1, 4), lax.rem(x + 3, 4), lax.rem(x + 2, 4)
    right, left = {"tensor": xr}, {"tensor": xl}
    scale = HEAD ** -0.5
    base2 = scale * LOG2E
    A, B = pl.ds(0, half), pl.ds(half, half)

    barrier = pltpu.get_barrier_semaphore()
    pl.semaphore_signal(barrier, inc=1, device_id=right, device_id_type=MESH)
    pl.semaphore_signal(barrier, inc=1, device_id=left, device_id_type=MESH)

    def greet(k, c):
        pl.semaphore_signal(barrier, inc=1, device_id={"replica": lax.rem(me + k, replicas)}, device_id_type=MESH)
        return c

    lax.fori_loop(1, replicas, greet, 0)

    loads = []

    def load(src, dst):
        copy = pltpu.make_async_copy(src, dst, lsem.at[len(loads)])
        copy.start()
        loads.append(copy)
        return copy

    l_dest, l_len = load(dest_hbm, dest_v), load(len_hbm, len_v)
    l_ga, l_gm = load(gain_a_hbm, gain_a), load(gain_m_hbm, gain_m)
    l_req, l_pro = load(request_hbm, rows_in.at[1, x]), load(prompt_hbm, rows_in.at[0, x])
    l_wq, l_wkv = load(wq_hbm, wq), load(wkv_hbm, wkv)
    l_prefix, l_cache = load(prefix_hbm, prefix), load(cache_hbm, cache)
    l_wo = [load(wo_hbm.at[:, pl.ds(d * width, width)], wo.at[d]) for d in range(4)]
    l_wg, l_wu = load(wg_hbm, wg), load(wu_hbm, wu)
    l_wd = [load(wd_hbm.at[:, pl.ds(d * width, width)], wd.at[d]) for d in range(4)]

    pl.semaphore_wait(barrier, replicas + 1)

    sent = []

    def ring(base, i, src, dst, to):
        copy = pltpu.make_async_remote_copy(
            src_ref=src, dst_ref=dst, send_sem=ssem.at[base + i], recv_sem=rsem.at[base + i],
            device_id=to, device_id_type=MESH)
        sent.append(copy)
        return copy

    def gather(base, own, whole):
        own_a, own_b = own
        return [
            ring(base, 0, own_a, whole.at[x, A], right), ring(base, 1, own_b, whole.at[x, B], left),
            ring(base, 2, own_b, whole.at[x, B], right), ring(base, 3, own_a, whole.at[x, A], left),
            ring(base, 4, whole.at[xl, A], whole.at[xl, A], right), ring(base, 5, whole.at[xr, B], whole.at[xr, B], left),
        ]

    def begin(msgs):
        for m in msgs[:4]:
            m.start()

    def forward(msgs):
        for i in range(2):
            msgs[i].wait_recv()
            msgs[4 + i].start()

    def arrived(msgs):
        for m in msgs[2:]:
            m.wait_recv()

    def scatter(base, s):
        t = terms.at[s]
        return [
            ring(base, 0, t.at[x2, A], far2.at[s, 0], right), ring(base, 1, t.at[x2, B], far2.at[s, 1], left),
            ring(base, 2, t.at[xr, B], from_l.at[s, B], right), ring(base, 3, t.at[xl, A], from_r.at[s, A], left),
            ring(base, 4, folded.at[s, 0], from_l.at[s, A], right), ring(base, 5, folded.at[s, 1], from_r.at[s, B], left),
        ]

    def spread(msgs, s, make):
        terms[s, x2] = make(x2).astype(BF)
        msgs[0].start()
        msgs[1].start()
        terms[s, xr] = make(xr).astype(BF)
        msgs[2].start()
        terms[s, xl] = make(xl).astype(BF)
        msgs[3].start()
        terms[s, x] = make(x).astype(BF)

    def fold(msgs, s):
        for i, part in enumerate(((xr, A), (xl, B))):
            msgs[i].wait_recv()
            folded[s, i] = (terms[s, part[0], part[1]].astype(F32) + far2[s, i].astype(F32)).astype(BF)
            msgs[4 + i].start()

    def summed(msgs, s):
        for m in msgs[2:]:
            m.wait_recv()
        return terms[s, x].astype(F32) + (from_l[s].astype(F32) + from_r[s].astype(F32))

    g_req = gather(0, (request_hbm.at[A], request_hbm.at[B]), rows_in.at[1])
    g_pro = gather(6, (prompt_hbm.at[A], prompt_hbm.at[B]), rows_in.at[0])
    begin(g_req)

    n = dest_v.shape[1]
    l_dest.wait()
    eye = lax.broadcasted_iota(jnp.int32, (n, n), 0) - lax.broadcasted_iota(jnp.int32, (n, n), 1)
    dest_row = dest_v[...].astype(F32)
    dest_mat = jnp.broadcast_to(dest_row, (n, n))
    dest_col = jnp.sum(jnp.where(eye == 0, dest_mat, 0.0), axis=1, keepdims=True)
    same = dest_mat == jnp.broadcast_to(dest_col, (n, n))
    rank_col = jnp.sum(jnp.where(same & (eye > 0), 1.0, 0.0), axis=1, keepdims=True)
    rank_row = jnp.sum(jnp.where(same & (eye < 0), 1.0, 0.0), axis=0, keepdims=True)
    me_f = me.astype(F32)
    turn = replicas * 3 // 8
    home = replicas - turn

    def block_of(dest):
        gap = dest - me_f - turn
        gap = jnp.where(gap < 0, gap + replicas, gap)
        return jnp.where(gap < 0, gap + replicas, gap)

    put_row = block_of(dest_row) * 8 + rank_row
    put_row = jnp.concatenate((put_row, put_row + 4), axis=1)
    slots = replicas * 8
    put[...] = jnp.where(
        jnp.broadcast_to(put_row, (slots, 2 * n)) == lax.broadcasted_iota(jnp.int32, (slots, 2 * n), 0).astype(F32),
        1.0, 0.0).astype(BF)
    take_col = block_of(dest_col) * 16 + rank_col
    take_col = jnp.concatenate((take_col, take_col + 4, take_col + 8, take_col + 12), axis=0)
    take[...] = jnp.where(
        jnp.broadcast_to(take_col, (4 * n, 2 * slots))
        == lax.broadcasted_iota(jnp.int32, (4 * n, 2 * slots), 1).astype(F32), 1.0, 0.0).astype(BF)

    l_prefix.wait()
    ones_prefix[...] = with_ones(prefix[...])
    l_len.wait()
    len_mat = jnp.broadcast_to(len_v[...].astype(F32), (n, n))
    len_col = jnp.sum(jnp.where(eye == 0, len_mat, 0.0), axis=1, keepdims=True)

    forward(g_req)
    begin(g_pro)
    l_ga.wait()
    l_wq.wait()
    l_wkv.wait()
    l_req.wait()
    arrived(g_req)

    def project(s):
        normed = norm([rows_in[s, d] for d in range(4)], gain_a[...])
        return dot(normed, wq[...]).astype(BF), dot(normed, wkv[...]).astype(BF)

    q_req, kv_req = project(1)
    stacked = jnp.concatenate((q_req[:, :128], q_req[:, 128:]), axis=0)
    q_rows[0] = stacked[:n].astype(F32)
    q_rows[1] = stacked[n:].astype(F32)
    q_send[...] = dot(put[...], stacked).reshape(replicas, 8, 128).astype(BF)

    per = replicas // 4
    runs = {0: (0, per), 1: (per, 2 * per), 2: (2 * per, home), 3: (3 * per, 4 * per), 4: (home + 1, 3 * per)}
    steps = ((0,), (1,), (3,), (2, 4))

    def travel(buf_out, buf_in, kk, sem, sign):
        return pltpu.make_async_remote_copy(
            src_ref=buf_out.at[kk], dst_ref=buf_in.at[kk], send_sem=xsend.at[sem], recv_sem=xrecv.at[sem],
            device_id={"replica": lax.rem(me + 2 * replicas + sign * (kk + turn), replicas)}, device_id_type=MESH)

    def launch(buf_out, buf_in, run, sem, sign):
        def one(kk, c):
            travel(buf_out, buf_in, kk, sem, sign).start()
            return c
        lax.fori_loop(runs[run][0], runs[run][1], one, 0)

    def whole_run(buf_out, buf_in, run, sem):
        part = pl.ds(runs[run][0], runs[run][1] - runs[run][0])
        return pltpu.make_async_remote_copy(
            src_ref=buf_out.at[part], dst_ref=buf_in.at[part], send_sem=xsend.at[sem], recv_sem=xrecv.at[sem],
            device_id={"replica": lax.rem(me + 1, replicas)}, device_id_type=MESH)

    for step in steps:
        for run in step:
            launch(q_send, q_recv, run, run, 1)
    q_recv[home] = q_send[home]
    forward(g_pro)

    l_cache.wait()
    group = 8
    cols = group * cache.shape[1]
    row_id = lax.broadcasted_iota(jnp.int32, (group, cols), 0)
    col_id = lax.broadcasted_iota(jnp.int32, (group, cols), 1)
    position = (col_id - row_id * cache.shape[1]).astype(F32)
    def cached_part(g):
        part = slice(g * group, (g + 1) * group)
        q4 = jnp.concatenate([split_heads(q_rows[hp, part]) for hp in range(2)], axis=0)
        keys = cache[part].reshape(cols, 128)
        alive = (position >= 0) & (position < jnp.broadcast_to(len_col[part], (group, cols)))
        alive = jnp.concatenate((alive,) * 4, axis=0)
        scores = jnp.where(alive, dot_t(q4, keys), -jnp.inf)
        top = jnp.max(scores, axis=1, keepdims=True)
        weights = jnp.exp2(scores * base2 - top * base2).astype(BF)
        mixed = dot(weights, with_ones(keys))
        for hp in range(2):
            joined = join_heads(mixed[hp * 2 * group:(hp + 1) * 2 * group], top[hp * 2 * group:(hp + 1) * 2 * group])
            for i in range(3):
                past[i, hp, part] = joined[i]

    for g in range(12):
        cached_part(g)

    def attend(q, local=None):
        scores = dot_t(q, prefix[...])
        top = jnp.max(scores, axis=1, keepdims=True)
        if local is not None:
            near = dot_t(q, local)
            m = near.shape[1]
            seen = (lax.broadcasted_iota(jnp.int32, near.shape, 1)
                    <= lax.rem(lax.broadcasted_iota(jnp.int32, near.shape, 0), m))
            near = jnp.where(seen, near, -jnp.inf)
            top = jnp.maximum(top, jnp.max(near, axis=1, keepdims=True))
        shift = top * base2
        mixed = dot(jnp.exp2(scores * base2 - shift).astype(BF), ones_prefix[...])
        if local is not None:
            mixed = mixed + dot(jnp.exp2(near * base2 - shift).astype(BF), with_ones(local))
        return join_heads(mixed, top)

    l_pro.wait()
    arrived(g_pro)
    q_pro, kv_pro = project(0)
    for hp in range(2):
        above, total, _ = attend(split_heads(q_pro[:, hp * 128:(hp + 1) * 128].astype(F32)), kv_pro)
        att[0, :, hp * 128:(hp + 1) * 128] = (above / total).astype(BF)

    for c in l_wo:
        c.wait()
    s_pro = scatter(12, 0)
    spread(s_pro, 0, lambda d: dot(att[0], wo[d]))

    lane = lax.rem(lax.broadcasted_iota(jnp.int32, (per * 8, 128), 1), HEAD)

    def serve(step):
        first = min(runs[run][0] for run in steps[step])
        for run in steps[step]:
            whole_run(q_send, q_recv, run, run).wait_recv()
        rows = q_recv[first:first + per].astype(F32).reshape(per * 8, 128)
        above, total, top = attend(split_heads(rows))
        level = top * scale + jnp.log(total)
        hi = level.astype(BF).astype(F32)
        mid_part = (level - hi).astype(BF).astype(F32)
        lo = level - hi - mid_part
        stat = jnp.where(lane < 16, hi, jnp.where(lane < 32, mid_part, lo))
        packed = jnp.concatenate(
            ((above / total).reshape(per, 8, 128), stat.reshape(per, 8, 128)), axis=1)
        r_send[first:first + per] = packed.astype(BF)
        for run in steps[step]:
            launch(r_send, r_recv, run, 5 + run, -1)

    def settle(msgs, s):
        row = rows_in[s, x].astype(F32)
        mid[s, x] = (row + summed(msgs, s)).astype(BF)
        return None

    def feed(base, s):
        own = mid.at[s, x]
        return gather(base, (own.at[A], own.at[B]), mid.at[s])

    def hidden_of(s):
        normed = norm([mid[s, d] for d in range(4)], gain_m[...])
        gate = dot(normed, wg[...])
        up = dot(normed, wu[...])
        return (gate / (1.0 + jnp.exp(-gate)) * up).astype(BF)

    serve(0)
    serve(1)
    fold(s_pro, 0)
    serve(2)
    serve(3)
    r_recv[home] = r_send[home]
    for g in range(12, 16):
        cached_part(g)
    settle(s_pro, 0)
    m_pro = feed(18, 0)
    begin(m_pro)

    for step in steps:
        for run in step:
            whole_run(r_send, r_recv, run, 5 + run).wait_recv()
    back = dot(take[...], r_recv[...].reshape(2 * slots, 128))
    far_mix = back[:2 * n]
    e_row = lax.broadcasted_iota(jnp.int32, (128, 128), 0)
    e_col = lax.broadcasted_iota(jnp.int32, (128, 128), 1)
    pick = ((e_row < HEAD) == (e_col < HEAD)) & (
        (lax.rem(e_row, HEAD) == 0) | (lax.rem(e_row, HEAD) == 16) | (lax.rem(e_row, HEAD) == 32))
    far_level = dot(back[2 * n:].astype(BF), jnp.where(pick, 1.0, 0.0).astype(BF))
    q2 = q_rows[...].reshape(2 * n, 128)
    kv = kv_req.astype(F32)
    low = low_lanes(kv.shape)
    key2 = jnp.where(low, kv, swap(kv))
    val2 = jnp.where(low, swap(kv), kv)
    key2 = jnp.concatenate((key2, key2), axis=0)
    val2 = jnp.concatenate((val2, val2), axis=0)
    prod = q2 * key2
    low2 = low_lanes(prod.shape)
    own_even = jnp.sum(jnp.where(low2, prod, 0.0), axis=1, keepdims=True)
    own_odd = jnp.sum(jnp.where(low2, 0.0, prod), axis=1, keepdims=True)
    own = jnp.where(low2, jnp.broadcast_to(own_even, prod.shape), jnp.broadcast_to(own_odd, prod.shape)) * scale
    p_mix, p_total, p_top = past[0].reshape(2 * n, 128), past[1].reshape(2 * n, 128), past[2].reshape(2 * n, 128) * scale
    top = jnp.maximum(jnp.maximum(far_level, p_top), own)
    w_far, w_past, w_own = jnp.exp(far_level - top), jnp.exp(p_top - top), jnp.exp(own - top)
    merged = (far_mix * w_far + p_mix * w_past + val2 * w_own) / (w_far + p_total * w_past + w_own)
    att[1] = jnp.concatenate((merged[:n], merged[n:]), axis=1).astype(BF)

    s_req = scatter(30, 1)
    spread(s_req, 1, lambda d: dot(att[1], wo[d]))
    forward(m_pro)
    fold(s_req, 1)
    l_gm.wait()
    l_wg.wait()
    l_wu.wait()
    for c in l_wd:
        c.wait()
    settle(s_req, 1)
    m_req = feed(36, 1)
    begin(m_req)
    arrived(m_pro)
    hid = hidden_of(0)
    d_pro = scatter(24, 2)
    spread(d_pro, 2, lambda d: dot(hid, wd[d]))
    forward(m_req)
    fold(d_pro, 2)
    arrived(m_req)
    hid_r = hidden_of(1)
    d_req = scatter(42, 3)
    spread(d_req, 3, lambda d: dot(hid_r, wd[d]))
    prompt_out[...] = (mid[0, x].astype(F32) + summed(d_pro, 2)).astype(BF)
    fold(d_req, 3)
    request_out[...] = (mid[1, x].astype(F32) + summed(d_req, 3)).astype(BF)

    for c in sent:
        c.wait_send()
    for run in runs:
        whole_run(q_send, q_recv, run, run).wait_send()
        whole_run(r_send, r_recv, run, 5 + run).wait_send()


def hand_over(a, b, c, d):
    c[...] = a[...]
    d[...] = b[...]


def body(
    prompt_rows, request_rows, request_keyval_cache, cache_len, destination, prefix_cache,
    attn_gain, w_query, keyval_weight, w_out, mlp_gain, w_gate, w_up, w_down,
):
    replicas = lax.axis_size("replica")
    n, width = request_rows.shape
    model = w_query.shape[0]
    units = w_gate.shape[1]
    cached = request_keyval_cache.shape[1]
    pre = prefix_cache.shape[0]
    V = pltpu.VMEM
    DMA = pltpu.SemaphoreType.DMA
    out = jax.ShapeDtypeStruct((n, width), BF)
    anyspec = pl.BlockSpec(memory_space=pl.ANY)
    vspec = pl.BlockSpec(memory_space=pltpu.VMEM)
    half = n // 2
    held = pl.pallas_call(
        functools.partial(kernel, replicas),
        out_shape=(out, out),
        in_specs=[anyspec] * 14,
        out_specs=(vspec, vspec),
        scratch_shapes=[
            V((1, n), jnp.int32), V((1, n), jnp.int32), V((1, model), F32), V((1, model), F32),
            V((2, 4, n, width), BF), V((2, 4, n, width), BF),
            V((pre, 128), BF), V((pre, 128), BF), V((n, cached, 128), BF),
            V((model, 256), BF), V((model, 128), BF), V((4, 256, width), BF),
            V((model, units), BF), V((model, units), BF), V((4, units, width), BF),
            V((replicas * 8, 2 * n), BF), V((4 * n, replicas * 16), BF), V((2, n, 128), F32),
            V((replicas, 8, 128), BF), V((replicas, 8, 128), BF),
            V((replicas, 16, 128), BF), V((replicas, 16, 128), BF),
            V((3, 2, n, 128), F32), V((8, 128), BF),
            V((4, 4, n, width), BF), V((4, 2, half, width), BF),
            V((4, n, width), BF), V((4, n, width), BF), V((4, 2, half, width), BF), V((2, n, 256), BF),
            DMA((20,)), DMA((48,)), DMA((48,)), DMA((10,)), DMA((10,)),
        ],
        compiler_params=pltpu.CompilerParams(
            collective_id=0, has_side_effects=True, vmem_limit_bytes=60 * 1024 * 1024),
    )(
        prompt_rows, request_rows, request_keyval_cache, cache_len.reshape(1, n), destination.reshape(1, n), prefix_cache,
        attn_gain.reshape(1, model), w_query, keyval_weight, w_out, mlp_gain.reshape(1, model), w_gate, w_up, w_down,
    )
    return pl.pallas_call(
        hand_over, out_shape=(out, out), in_specs=[vspec, vspec], out_specs=(vspec, vspec))(*held)


def solution(mesh):
    return jax.shard_map(
        body,
        mesh=mesh,
        in_specs=(
            P("replica", "tensor"), P("replica", "tensor"), P("replica", None, "tensor"), P("replica"),
            P("replica", None), P("replica", "tensor"), P(), P(None, "tensor"), P(None, "tensor"),
            P("tensor", None), P(), P(None, "tensor"), P(None, "tensor"), P("tensor", None),
        ),
        out_specs=(P("replica", "tensor"), P("replica", "tensor")),
        check_vma=False,
    )
```

```python
import functools
import math

import jax
import jax.numpy as jnp
from jax import lax
from jax.experimental import pallas as pl
from jax.experimental.pallas import tpu as pltpu
from jax.sharding import PartitionSpec as P

HEAD = 64
EPS = 1e-05
BF = jnp.bfloat16
F32 = jnp.float32
MESH = pl.DeviceIdType.MESH
LOG2E = math.log2(math.e)


def dot(a, b):
    return jnp.dot(a, b, preferred_element_type=F32)


def dot_t(a, b):
    return lax.dot_general(a, b, (((1,), (1,)), ((), ())), preferred_element_type=F32)


def low_lanes(shape):
    return lax.broadcasted_iota(jnp.int32, shape, len(shape) - 1) % 128 < HEAD


def swap(v):
    return pltpu.roll(v, HEAD, 1)


def split_heads(v):
    low = low_lanes(v.shape)
    return jnp.concatenate((jnp.where(low, v, 0.0), jnp.where(low, swap(v), 0.0)), axis=0).astype(BF)


def join_heads(mixed, top):
    n = mixed.shape[0] // 2
    even, odd = mixed[:n], mixed[n:]
    low = low_lanes(even.shape)
    return (
        jnp.where(low, swap(even), odd),
        jnp.where(low, even, swap(odd)),
        jnp.where(low, jnp.broadcast_to(top[:n], even.shape), jnp.broadcast_to(top[n:], even.shape)),
    )


def with_ones(keyval):
    return jnp.where(low_lanes(keyval.shape), jnp.ones_like(keyval), keyval)


def norm(pieces, gain):
    values = jnp.concatenate([p.astype(F32) for p in pieces], axis=1)
    inv_scale = lax.rsqrt(jnp.mean(values * values, axis=1, keepdims=True) + EPS)
    return (values * inv_scale * gain).astype(BF)


def kernel(
    replicas,
    prompt_hbm, request_hbm, cache_hbm, len_hbm, dest_hbm, prefix_hbm, gain_a_hbm, wq_hbm, wkv_hbm, wo_hbm,
    gain_m_hbm, wg_hbm, wu_hbm, wd_hbm,
    prompt_out, request_out,
    dest_v, len_v, gain_a, gain_m, rows_in, mid, prefix, ones_prefix, cache, wq, wkv, wo, wg, wu, wd,
    put, take, q_rows, q_send, q_recv, r_send, r_recv, past, res, terms, far2, from_l, from_r, folded, att, wsem, wrecv,
    lsem, ssem, rsem, xsend, xrecv,
):
    half, width = rows_in.shape[2] // 2, rows_in.shape[3]
    x = lax.axis_index("tensor")
    me = lax.axis_index("replica")
    xr, xl, x2 = lax.rem(x + 1, 4), lax.rem(x + 3, 4), lax.rem(x + 2, 4)
    right, left = {"tensor": xr}, {"tensor": xl}
    scale = HEAD ** -0.5
    base2 = scale * LOG2E
    A, B = pl.ds(0, half), pl.ds(half, half)

    barrier = pltpu.get_barrier_semaphore()
    pl.semaphore_signal(barrier, inc=1, device_id=right, device_id_type=MESH)
    pl.semaphore_signal(barrier, inc=1, device_id=left, device_id_type=MESH)

    def greet(k, c):
        pl.semaphore_signal(barrier, inc=1, device_id={"replica": lax.rem(me + k, replicas)}, device_id_type=MESH)
        return c

    lax.fori_loop(1, replicas, greet, 0)

    loads = []

    def load(src, dst):
        copy = pltpu.make_async_copy(src, dst, lsem.at[len(loads)])
        copy.start()
        loads.append(copy)
        return copy

    l_dest, l_len = load(dest_hbm, dest_v), load(len_hbm, len_v)
    l_ga, l_gm = load(gain_a_hbm, gain_a), load(gain_m_hbm, gain_m)
    l_req, l_pro = load(request_hbm, rows_in.at[1, x]), load(prompt_hbm, rows_in.at[0, x])
    l_wq, l_wkv = load(wq_hbm, wq), load(wkv_hbm, wkv)
    l_prefix, l_cache = load(prefix_hbm, prefix), load(cache_hbm, cache)
    part_rows = wo.shape[2]
    l_wo = [load(wo_hbm.at[pl.ds(c * part_rows, part_rows)], wo.at[c, x]) for c in range(2)]
    l_wg, l_wu = load(wg_hbm, wg), load(wu_hbm, wu)
    l_wd = [load(wd_hbm.at[:, pl.ds(d * width, width)], wd.at[d]) for d in range(4)]

    pl.semaphore_wait(barrier, replicas + 1)

    sent = []

    def ring(base, i, src, dst, to):
        copy = pltpu.make_async_remote_copy(
            src_ref=src, dst_ref=dst, send_sem=ssem.at[base + i], recv_sem=rsem.at[base + i],
            device_id=to, device_id_type=MESH)
        sent.append(copy)
        return copy

    def gather(base, own, whole):
        own_a, own_b = own
        return [
            ring(base, 0, own_a, whole.at[x, A], right), ring(base, 1, own_b, whole.at[x, B], left),
            ring(base, 2, own_b, whole.at[x, B], right), ring(base, 3, own_a, whole.at[x, A], left),
            ring(base, 4, whole.at[xl, A], whole.at[xl, A], right), ring(base, 5, whole.at[xr, B], whole.at[xr, B], left),
        ]

    def begin(msgs):
        for m in msgs[:4]:
            m.start()

    def forward(msgs):
        for i in range(2):
            msgs[i].wait_recv()
            msgs[4 + i].start()

    def arrived(msgs):
        for m in msgs[2:]:
            m.wait_recv()

    def scatter(base, s):
        t = terms.at[s]
        return [
            ring(base, 0, t.at[x2, A], far2.at[s, 0], right), ring(base, 1, t.at[x2, B], far2.at[s, 1], left),
            ring(base, 2, t.at[xr, B], from_l.at[s, B], right), ring(base, 3, t.at[xl, A], from_r.at[s, A], left),
            ring(base, 4, folded.at[s, 0], from_l.at[s, A], right), ring(base, 5, folded.at[s, 1], from_r.at[s, B], left),
        ]

    def spread(msgs, s, make):
        terms[s, x2] = make(x2).astype(BF)
        msgs[0].start()
        msgs[1].start()
        terms[s, xr] = make(xr).astype(BF)
        msgs[2].start()
        terms[s, xl] = make(xl).astype(BF)
        msgs[3].start()
        terms[s, x] = make(x).astype(BF)

    def fold(msgs, s):
        for i, part in enumerate(((xr, A), (xl, B))):
            msgs[i].wait_recv()
            folded[s, i] = (terms[s, part[0], part[1]].astype(F32) + far2[s, i].astype(F32)).astype(BF)
            msgs[4 + i].start()

    def summed(msgs, s):
        for m in msgs[2:]:
            m.wait_recv()
        return terms[s, x].astype(F32) + (from_l[s].astype(F32) + from_r[s].astype(F32))

    g_req = gather(0, (request_hbm.at[A], request_hbm.at[B]), rows_in.at[1])
    g_pro = gather(6, (prompt_hbm.at[A], prompt_hbm.at[B]), rows_in.at[0])
    core = lax.rem(me, 2)
    w_base = core * part_rows
    g_out = gather(
        12, (wo_hbm.at[pl.ds(w_base, half)], wo_hbm.at[pl.ds(w_base + half, half)]), wo.at[core])
    begin(g_req)

    n = dest_v.shape[1]
    l_dest.wait()
    eye = lax.broadcasted_iota(jnp.int32, (n, n), 0) - lax.broadcasted_iota(jnp.int32, (n, n), 1)
    dest_row = dest_v[...].astype(F32)
    dest_mat = jnp.broadcast_to(dest_row, (n, n))
    dest_col = jnp.sum(jnp.where(eye == 0, dest_mat, 0.0), axis=1, keepdims=True)
    same = dest_mat == jnp.broadcast_to(dest_col, (n, n))
    rank_col = jnp.sum(jnp.where(same & (eye > 0), 1.0, 0.0), axis=1, keepdims=True)
    rank_row = jnp.sum(jnp.where(same & (eye < 0), 1.0, 0.0), axis=0, keepdims=True)
    me_f = me.astype(F32)
    turn = replicas * 3 // 8
    home = replicas - turn

    def block_of(dest):
        gap = dest - me_f - turn
        gap = jnp.where(gap < 0, gap + replicas, gap)
        return jnp.where(gap < 0, gap + replicas, gap)

    put_row = block_of(dest_row) * 8 + rank_row
    put_row = jnp.concatenate((put_row, put_row + 4), axis=1)
    slots = replicas * 8
    put[...] = jnp.where(
        jnp.broadcast_to(put_row, (slots, 2 * n)) == lax.broadcasted_iota(jnp.int32, (slots, 2 * n), 0).astype(F32),
        1.0, 0.0).astype(BF)
    take_col = block_of(dest_col) * 16 + rank_col
    take_col = jnp.concatenate((take_col, take_col + 4, take_col + 8, take_col + 12), axis=0)
    take[...] = jnp.where(
        jnp.broadcast_to(take_col, (4 * n, 2 * slots))
        == lax.broadcasted_iota(jnp.int32, (4 * n, 2 * slots), 1).astype(F32), 1.0, 0.0).astype(BF)

    l_prefix.wait()
    ones_prefix[...] = with_ones(prefix[...])
    l_len.wait()
    len_mat = jnp.broadcast_to(len_v[...].astype(F32), (n, n))
    len_col = jnp.sum(jnp.where(eye == 0, len_mat, 0.0), axis=1, keepdims=True)

    forward(g_req)
    begin(g_pro)
    l_ga.wait()
    l_wq.wait()
    l_wkv.wait()
    l_req.wait()
    arrived(g_req)

    def project(s):
        normed = norm([rows_in[s, d] for d in range(4)], gain_a[...])
        return dot(normed, wq[...]).astype(BF), dot(normed, wkv[...]).astype(BF)

    q_req, kv_req = project(1)
    stacked = jnp.concatenate((q_req[:, :128], q_req[:, 128:]), axis=0)
    q_rows[0] = stacked[:n].astype(F32)
    q_rows[1] = stacked[n:].astype(F32)
    q_send[...] = dot(put[...], stacked).reshape(replicas, 8, 128).astype(BF)

    per = replicas // 4
    runs = {0: (0, per), 1: (per, 2 * per), 2: (2 * per, home), 3: (3 * per, 4 * per), 4: (home + 1, 3 * per)}
    steps = ((0,), (1,), (3,), (2, 4))

    def travel(buf_out, buf_in, kk, sem, sign):
        return pltpu.make_async_remote_copy(
            src_ref=buf_out.at[kk], dst_ref=buf_in.at[kk], send_sem=xsend.at[sem], recv_sem=xrecv.at[sem],
            device_id={"replica": lax.rem(me + 2 * replicas + sign * (kk + turn), replicas)}, device_id_type=MESH)

    def launch(buf_out, buf_in, run, sem, sign):
        def one(kk, c):
            travel(buf_out, buf_in, kk, sem, sign).start()
            return c
        lax.fori_loop(runs[run][0], runs[run][1], one, 0)

    def whole_run(buf_out, buf_in, run, sem):
        part = pl.ds(runs[run][0], runs[run][1] - runs[run][0])
        return pltpu.make_async_remote_copy(
            src_ref=buf_out.at[part], dst_ref=buf_in.at[part], send_sem=xsend.at[sem], recv_sem=xrecv.at[sem],
            device_id={"replica": lax.rem(me + 1, replicas)}, device_id_type=MESH)

    for step in steps:
        for run in step:
            launch(q_send, q_recv, run, run, 1)
    q_recv[home] = q_send[home]
    forward(g_pro)
    begin(g_out)

    l_cache.wait()
    group = 8
    cols = group * cache.shape[1]
    row_id = lax.broadcasted_iota(jnp.int32, (group, cols), 0)
    col_id = lax.broadcasted_iota(jnp.int32, (group, cols), 1)
    position = (col_id - row_id * cache.shape[1]).astype(F32)
    def cached_part(g):
        part = slice(g * group, (g + 1) * group)
        q4 = jnp.concatenate([split_heads(q_rows[hp, part]) for hp in range(2)], axis=0)
        keys = cache[part].reshape(cols, 128)
        alive = (position >= 0) & (position < jnp.broadcast_to(len_col[part], (group, cols)))
        alive = jnp.concatenate((alive,) * 4, axis=0)
        scores = jnp.where(alive, dot_t(q4, keys), -jnp.inf)
        top = jnp.max(scores, axis=1, keepdims=True)
        weights = jnp.exp2(scores * base2 - top * base2).astype(BF)
        mixed = dot(weights, with_ones(keys))
        for hp in range(2):
            joined = join_heads(mixed[hp * 2 * group:(hp + 1) * 2 * group], top[hp * 2 * group:(hp + 1) * 2 * group])
            for i in range(3):
                past[i, hp, part] = joined[i]

    for g in range(12):
        cached_part(g)

    def attend(q, local=None):
        scores = dot_t(q, prefix[...])
        top = jnp.max(scores, axis=1, keepdims=True)
        if local is not None:
            near = dot_t(q, local)
            m = near.shape[1]
            seen = (lax.broadcasted_iota(jnp.int32, near.shape, 1)
                    <= lax.rem(lax.broadcasted_iota(jnp.int32, near.shape, 0), m))
            near = jnp.where(seen, near, -jnp.inf)
            top = jnp.maximum(top, jnp.max(near, axis=1, keepdims=True))
        shift = top * base2
        mixed = dot(jnp.exp2(scores * base2 - shift).astype(BF), ones_prefix[...])
        if local is not None:
            mixed = mixed + dot(jnp.exp2(near * base2 - shift).astype(BF), with_ones(local))
        return join_heads(mixed, top)

    l_pro.wait()
    arrived(g_pro)
    q_pro, kv_pro = project(0)
    for hp in range(2):
        above, total, _ = attend(split_heads(q_pro[:, hp * 128:(hp + 1) * 128].astype(F32)), kv_pro)
        att[0, x, :, hp * 128:(hp + 1) * 128] = (above / total).astype(BF)

    def share(base, s):
        own = att.at[s, x]
        return gather(base, (own.at[A], own.at[B]), att.at[s])

    a_pro = share(18, 0)
    begin(a_pro)

    lane = lax.rem(lax.broadcasted_iota(jnp.int32, (per * 8, 128), 1), HEAD)

    def serve(step):
        first = min(runs[run][0] for run in steps[step])
        for run in steps[step]:
            whole_run(q_send, q_recv, run, run).wait_recv()
        rows = q_recv[first:first + per].astype(F32).reshape(per * 8, 128)
        above, total, top = attend(split_heads(rows))
        level = top * scale + jnp.log(total)
        hi = level.astype(BF).astype(F32)
        mid_part = (level - hi).astype(BF).astype(F32)
        lo = level - hi - mid_part
        stat = jnp.where(lane < 16, hi, jnp.where(lane < 32, mid_part, lo))
        packed = jnp.concatenate(
            ((above / total).reshape(per, 8, 128), stat.reshape(per, 8, 128)), axis=1)
        r_send[first:first + per] = packed.astype(BF)
        for run in steps[step]:
            launch(r_send, r_recv, run, 5 + run, -1)

    def sibling(i, quarter):
        return pltpu.make_async_remote_copy(
            src_ref=wo.at[core, quarter], dst_ref=wo.at[core, quarter], send_sem=wsem.at[i], recv_sem=wrecv.at[i],
            device_id={"replica": me + 1 - 2 * core}, device_id_type=MESH)

    def settle(s):
        for d in range(4):
            cols = slice(d * width, (d + 1) * width)
            mixed = 0.0
            for g in range(4):
                both = dot(att[s, g, :, :128], wo[0, g, :, cols]) + dot(att[s, g, :, 128:], wo[1, g, :, cols])
                mixed = mixed + both.astype(BF).astype(F32)
            mid[s, d] = (rows_in[s, d].astype(F32) + mixed).astype(BF)

    def hidden_of(s):
        normed = norm([mid[s, d] for d in range(4)], gain_m[...])
        gate = dot(normed, wg[...])
        up = dot(normed, wu[...])
        return (gate / (1.0 + jnp.exp(-gate)) * up).astype(BF)

    serve(0)
    serve(1)
    forward(a_pro)
    serve(2)
    serve(3)
    r_recv[home] = r_send[home]
    for g in range(12, 16):
        cached_part(g)
    forward(g_out)
    arrived(a_pro)

    for step in steps:
        for run in step:
            whole_run(r_send, r_recv, run, 5 + run).wait_recv()
    back = dot(take[...], r_recv[...].reshape(2 * slots, 128))
    far_mix = back[:2 * n]
    e_row = lax.broadcasted_iota(jnp.int32, (128, 128), 0)
    e_col = lax.broadcasted_iota(jnp.int32, (128, 128), 1)
    pick = ((e_row < HEAD) == (e_col < HEAD)) & (
        (lax.rem(e_row, HEAD) == 0) | (lax.rem(e_row, HEAD) == 16) | (lax.rem(e_row, HEAD) == 32))
    far_level = dot(back[2 * n:].astype(BF), jnp.where(pick, 1.0, 0.0).astype(BF))
    q2 = q_rows[...].reshape(2 * n, 128)
    kv = kv_req.astype(F32)
    low = low_lanes(kv.shape)
    key2 = jnp.where(low, kv, swap(kv))
    val2 = jnp.where(low, swap(kv), kv)
    key2 = jnp.concatenate((key2, key2), axis=0)
    val2 = jnp.concatenate((val2, val2), axis=0)
    prod = q2 * key2
    low2 = low_lanes(prod.shape)
    own_even = jnp.sum(jnp.where(low2, prod, 0.0), axis=1, keepdims=True)
    own_odd = jnp.sum(jnp.where(low2, 0.0, prod), axis=1, keepdims=True)
    own = jnp.where(low2, jnp.broadcast_to(own_even, prod.shape), jnp.broadcast_to(own_odd, prod.shape)) * scale
    p_mix, p_total, p_top = past[0].reshape(2 * n, 128), past[1].reshape(2 * n, 128), past[2].reshape(2 * n, 128) * scale
    top = jnp.maximum(jnp.maximum(far_level, p_top), own)
    w_far, w_past, w_own = jnp.exp(far_level - top), jnp.exp(p_top - top), jnp.exp(own - top)
    merged = (far_mix * w_far + p_mix * w_past + val2 * w_own) / (w_far + p_total * w_past + w_own)
    att[1, x] = jnp.concatenate((merged[:n], merged[n:]), axis=1).astype(BF)

    a_req = share(24, 1)
    begin(a_req)
    siblings = [sibling(0, xl), sibling(1, xr), sibling(2, x2)]
    g_out[2].wait_recv()
    siblings[0].start()
    g_out[3].wait_recv()
    siblings[1].start()
    for c in l_wo:
        c.wait()
    l_gm.wait()
    l_wg.wait()
    l_wu.wait()
    for c in l_wd:
        c.wait()
    forward(a_req)
    g_out[4].wait_recv()
    g_out[5].wait_recv()
    siblings[2].start()
    arrived(a_req)
    for c in siblings:
        c.wait_recv()
    settle(1)
    hid_r = hidden_of(1)
    d_req = scatter(30, 1)
    spread(d_req, 1, lambda d: dot(hid_r, wd[d]))
    settle(0)
    hid = hidden_of(0)
    d_pro = scatter(36, 0)
    fold(d_req, 1)
    spread(d_pro, 0, lambda d: dot(hid, wd[d]))
    fold(d_pro, 0)
    request_out[...] = (mid[1, x].astype(F32) + summed(d_req, 1)).astype(BF)
    prompt_out[...] = (mid[0, x].astype(F32) + summed(d_pro, 0)).astype(BF)

    for c in siblings:
        c.wait_send()
    for c in sent:
        c.wait_send()
    for run in runs:
        whole_run(q_send, q_recv, run, run).wait_send()
        whole_run(r_send, r_recv, run, 5 + run).wait_send()


def hand_over(a, b, c, d):
    c[...] = a[...]
    d[...] = b[...]


def body(
    prompt_rows, request_rows, request_keyval_cache, cache_len, destination, prefix_cache,
    attn_gain, w_query, keyval_weight, w_out, mlp_gain, w_gate, w_up, w_down,
):
    replicas = lax.axis_size("replica")
    n, width = request_rows.shape
    model = w_query.shape[0]
    units = w_gate.shape[1]
    cached = request_keyval_cache.shape[1]
    pre = prefix_cache.shape[0]
    V = pltpu.VMEM
    DMA = pltpu.SemaphoreType.DMA
    out = jax.ShapeDtypeStruct((n, width), BF)
    anyspec = pl.BlockSpec(memory_space=pl.ANY)
    vspec = pl.BlockSpec(memory_space=pltpu.VMEM)
    half = n // 2
    held = pl.pallas_call(
        functools.partial(kernel, replicas),
        out_shape=(out, out),
        in_specs=[anyspec] * 14,
        out_specs=(vspec, vspec),
        scratch_shapes=[
            V((1, n), jnp.int32), V((1, n), jnp.int32), V((1, model), F32), V((1, model), F32),
            V((2, 4, n, width), BF), V((2, 4, n, width), BF),
            V((pre, 128), BF), V((pre, 128), BF), V((n, cached, 128), BF),
            V((model, 256), BF), V((model, 128), BF), V((2, 4, n, model), BF),
            V((model, units), BF), V((model, units), BF), V((4, units, width), BF),
            V((replicas * 8, 2 * n), BF), V((4 * n, replicas * 16), BF), V((2, n, 128), F32),
            V((replicas, 8, 128), BF), V((replicas, 8, 128), BF),
            V((replicas, 16, 128), BF), V((replicas, 16, 128), BF),
            V((3, 2, n, 128), F32), V((8, 128), BF),
            V((2, 4, n, width), BF), V((2, 2, half, width), BF),
            V((2, n, width), BF), V((2, n, width), BF), V((2, 2, half, width), BF), V((2, 4, n, 256), BF), DMA((3,)), DMA((3,)),
            DMA((20,)), DMA((42,)), DMA((42,)), DMA((10,)), DMA((10,)),
        ],
        compiler_params=pltpu.CompilerParams(
            collective_id=0, has_side_effects=True, vmem_limit_bytes=60 * 1024 * 1024),
    )(
        prompt_rows, request_rows, request_keyval_cache, cache_len.reshape(1, n), destination.reshape(1, n), prefix_cache,
        attn_gain.reshape(1, model), w_query, keyval_weight, w_out, mlp_gain.reshape(1, model), w_gate, w_up, w_down,
    )
    return pl.pallas_call(
        hand_over, out_shape=(out, out), in_specs=[vspec, vspec], out_specs=(vspec, vspec))(*held)


def solution(mesh):
    return jax.shard_map(
        body,
        mesh=mesh,
        in_specs=(
            P("replica", "tensor"), P("replica", "tensor"), P("replica", None, "tensor"), P("replica"),
            P("replica", None), P("replica", "tensor"), P(), P(None, "tensor"), P(None, "tensor"),
            P("tensor", None), P(), P(None, "tensor"), P(None, "tensor"), P("tensor", None),
        ),
        out_specs=(P("replica", "tensor"), P("replica", "tensor")),
        check_vma=False,
    )
```

```python
import functools
import math

import jax
import jax.numpy as jnp
from jax import lax
from jax.experimental import pallas as pl
from jax.experimental.pallas import tpu as pltpu
from jax.sharding import PartitionSpec as P

HEAD = 64
EPS = 1e-05
BF = jnp.bfloat16
F32 = jnp.float32
MESH = pl.DeviceIdType.MESH
LOG2E = math.log2(math.e)


def dot(a, b):
    return jnp.dot(a, b, preferred_element_type=F32)


def dot_t(a, b):
    return lax.dot_general(a, b, (((1,), (1,)), ((), ())), preferred_element_type=F32)


def low_lanes(shape):
    return lax.broadcasted_iota(jnp.int32, shape, len(shape) - 1) % 128 < HEAD


def swap(v):
    return pltpu.roll(v, HEAD, 1)


def split_heads(v):
    low = low_lanes(v.shape)
    return jnp.concatenate((jnp.where(low, v, 0.0), jnp.where(low, swap(v), 0.0)), axis=0).astype(BF)


def join_heads(mixed, top):
    n = mixed.shape[0] // 2
    even, odd = mixed[:n], mixed[n:]
    low = low_lanes(even.shape)
    return (
        jnp.where(low, swap(even), odd),
        jnp.where(low, even, swap(odd)),
        jnp.where(low, jnp.broadcast_to(top[:n], even.shape), jnp.broadcast_to(top[n:], even.shape)),
    )


def with_ones(keyval):
    return jnp.where(low_lanes(keyval.shape), jnp.ones_like(keyval), keyval)


def norm(pieces, gain):
    values = jnp.concatenate([p.astype(F32) for p in pieces], axis=1)
    inv_scale = lax.rsqrt(jnp.mean(values * values, axis=1, keepdims=True) + EPS)
    return (values * inv_scale * gain).astype(BF)


def kernel(
    replicas,
    prompt_hbm, request_hbm, cache_hbm, len_hbm, dest_hbm, prefix_hbm, gain_a_hbm, wq_hbm, wkv_hbm, wo_hbm,
    gain_m_hbm, wg_hbm, wu_hbm, wd_hbm,
    prompt_out, request_out,
    dest_v, len_v, gain_a, gain_m, rows_in, mid, prefix, ones_prefix, cache, wq, wkv, wo, wg, wu, wd,
    put, take, q_rows, q_send, q_recv, r_send, r_recv, past, res, terms, far2, from_l, from_r, folded, att, wsem, wrecv,
    lsem, ssem, rsem, xsend, xrecv,
):
    half, width = rows_in.shape[2] // 2, rows_in.shape[3]
    x = lax.axis_index("tensor")
    me = lax.axis_index("replica")
    xr, xl, x2 = lax.rem(x + 1, 4), lax.rem(x + 3, 4), lax.rem(x + 2, 4)
    right, left = {"tensor": xr}, {"tensor": xl}
    scale = HEAD ** -0.5
    base2 = scale * LOG2E
    A, B = pl.ds(0, half), pl.ds(half, half)

    barrier = pltpu.get_barrier_semaphore()
    pl.semaphore_signal(barrier, inc=1, device_id=right, device_id_type=MESH)
    pl.semaphore_signal(barrier, inc=1, device_id=left, device_id_type=MESH)

    def greet(k, c):
        pl.semaphore_signal(barrier, inc=1, device_id={"replica": lax.rem(me + k, replicas)}, device_id_type=MESH)
        return c

    lax.fori_loop(1, replicas, greet, 0)

    loads = []

    def load(src, dst):
        copy = pltpu.make_async_copy(src, dst, lsem.at[len(loads)])
        copy.start()
        loads.append(copy)
        return copy

    l_dest, l_len = load(dest_hbm, dest_v), load(len_hbm, len_v)
    l_ga, l_gm = load(gain_a_hbm, gain_a), load(gain_m_hbm, gain_m)
    l_req, l_pro = load(request_hbm, rows_in.at[1, x]), load(prompt_hbm, rows_in.at[0, x])
    l_wq, l_wkv = load(wq_hbm, wq), load(wkv_hbm, wkv)
    l_prefix, l_cache = load(prefix_hbm, prefix), load(cache_hbm, cache)
    part_rows = wo.shape[1] // 2
    l_wo = [load(wo_hbm, wo.at[x])]
    l_wg, l_wu = load(wg_hbm, wg), load(wu_hbm, wu)
    l_wd = [load(wd_hbm.at[:, pl.ds(d * width, width)], wd.at[d]) for d in range(4)]

    pl.semaphore_wait(barrier, replicas + 1)

    sent = []

    def ring(base, i, src, dst, to):
        copy = pltpu.make_async_remote_copy(
            src_ref=src, dst_ref=dst, send_sem=ssem.at[base + i], recv_sem=rsem.at[base + i],
            device_id=to, device_id_type=MESH)
        sent.append(copy)
        return copy

    def gather(base, own, whole):
        own_a, own_b = own
        return [
            ring(base, 0, own_a, whole.at[x, A], right), ring(base, 1, own_b, whole.at[x, B], left),
            ring(base, 2, own_b, whole.at[x, B], right), ring(base, 3, own_a, whole.at[x, A], left),
            ring(base, 4, whole.at[xl, A], whole.at[xl, A], right), ring(base, 5, whole.at[xr, B], whole.at[xr, B], left),
        ]

    def begin(msgs):
        for m in msgs[:4]:
            m.start()

    def forward(msgs):
        for i in range(2):
            msgs[i].wait_recv()
            msgs[4 + i].start()

    def arrived(msgs):
        for m in msgs[2:]:
            m.wait_recv()

    def scatter(base, s):
        t = terms.at[s]
        return [
            ring(base, 0, t.at[x2, A], far2.at[s, 0], right), ring(base, 1, t.at[x2, B], far2.at[s, 1], left),
            ring(base, 2, t.at[xr, B], from_l.at[s, B], right), ring(base, 3, t.at[xl, A], from_r.at[s, A], left),
            ring(base, 4, folded.at[s, 0], from_l.at[s, A], right), ring(base, 5, folded.at[s, 1], from_r.at[s, B], left),
        ]

    def spread(msgs, s, make):
        terms[s, x2] = make(x2).astype(BF)
        msgs[0].start()
        msgs[1].start()
        terms[s, xr] = make(xr).astype(BF)
        msgs[2].start()
        terms[s, xl] = make(xl).astype(BF)
        msgs[3].start()
        terms[s, x] = make(x).astype(BF)

    def fold(msgs, s):
        for i, part in enumerate(((xr, A), (xl, B))):
            msgs[i].wait_recv()
            folded[s, i] = (terms[s, part[0], part[1]].astype(F32) + far2[s, i].astype(F32)).astype(BF)
            msgs[4 + i].start()

    def summed(msgs, s):
        for m in msgs[2:]:
            m.wait_recv()
        return terms[s, x].astype(F32) + (from_l[s].astype(F32) + from_r[s].astype(F32))

    g_req = gather(0, (request_hbm.at[A], request_hbm.at[B]), rows_in.at[1])
    g_pro = gather(6, (prompt_hbm.at[A], prompt_hbm.at[B]), rows_in.at[0])
    core = lax.rem(me, 2)
    w_base = pl.multiple_of(core * part_rows, part_rows)
    w_part = wo.at[:, pl.ds(w_base, part_rows)]
    g_out = gather(
        12, (wo_hbm.at[pl.ds(w_base, half)], wo_hbm.at[pl.ds(w_base + half, half)]), w_part)
    begin(g_req)

    n = dest_v.shape[1]
    l_dest.wait()
    eye = lax.broadcasted_iota(jnp.int32, (n, n), 0) - lax.broadcasted_iota(jnp.int32, (n, n), 1)
    dest_row = dest_v[...].astype(F32)
    dest_mat = jnp.broadcast_to(dest_row, (n, n))
    dest_col = jnp.sum(jnp.where(eye == 0, dest_mat, 0.0), axis=1, keepdims=True)
    same = dest_mat == jnp.broadcast_to(dest_col, (n, n))
    rank_col = jnp.sum(jnp.where(same & (eye > 0), 1.0, 0.0), axis=1, keepdims=True)
    rank_row = jnp.sum(jnp.where(same & (eye < 0), 1.0, 0.0), axis=0, keepdims=True)
    me_f = me.astype(F32)
    turn = replicas * 3 // 8
    home = replicas - turn

    def block_of(dest):
        gap = dest - me_f - turn
        gap = jnp.where(gap < 0, gap + replicas, gap)
        return jnp.where(gap < 0, gap + replicas, gap)

    put_row = block_of(dest_row) * 8 + rank_row
    put_row = jnp.concatenate((put_row, put_row + 4), axis=1)
    slots = replicas * 8
    put[...] = jnp.where(
        jnp.broadcast_to(put_row, (slots, 2 * n)) == lax.broadcasted_iota(jnp.int32, (slots, 2 * n), 0).astype(F32),
        1.0, 0.0).astype(BF)
    take_col = block_of(dest_col) * 16 + rank_col
    take_col = jnp.concatenate((take_col, take_col + 4, take_col + 8, take_col + 12), axis=0)
    take[...] = jnp.where(
        jnp.broadcast_to(take_col, (4 * n, 2 * slots))
        == lax.broadcasted_iota(jnp.int32, (4 * n, 2 * slots), 1).astype(F32), 1.0, 0.0).astype(BF)

    l_prefix.wait()
    ones_prefix[...] = with_ones(prefix[...])
    l_len.wait()
    len_mat = jnp.broadcast_to(len_v[...].astype(F32), (n, n))
    len_col = jnp.sum(jnp.where(eye == 0, len_mat, 0.0), axis=1, keepdims=True)

    forward(g_req)
    begin(g_pro)
    l_ga.wait()
    l_wq.wait()
    l_wkv.wait()
    l_req.wait()
    arrived(g_req)

    def project(s):
        normed = norm([rows_in[s, d] for d in range(4)], gain_a[...])
        return dot(normed, wq[...]).astype(BF), dot(normed, wkv[...]).astype(BF)

    q_req, kv_req = project(1)
    stacked = jnp.concatenate((q_req[:, :128], q_req[:, 128:]), axis=0)
    q_rows[0] = stacked[:n].astype(F32)
    q_rows[1] = stacked[n:].astype(F32)
    q_send[...] = dot(put[...], stacked).reshape(replicas, 8, 128).astype(BF)

    per = replicas // 4
    runs = {0: (0, per), 1: (per, 2 * per), 2: (2 * per, home), 3: (3 * per, 4 * per), 4: (home + 1, 3 * per)}
    steps = ((0,), (1,), (3,), (2, 4))

    def travel(buf_out, buf_in, kk, sem, sign):
        return pltpu.make_async_remote_copy(
            src_ref=buf_out.at[kk], dst_ref=buf_in.at[kk], send_sem=xsend.at[sem], recv_sem=xrecv.at[sem],
            device_id={"replica": lax.rem(me + 2 * replicas + sign * (kk + turn), replicas)}, device_id_type=MESH)

    def launch(buf_out, buf_in, run, sem, sign):
        def one(kk, c):
            travel(buf_out, buf_in, kk, sem, sign).start()
            return c
        lax.fori_loop(runs[run][0], runs[run][1], one, 0)

    def whole_run(buf_out, buf_in, run, sem):
        part = pl.ds(runs[run][0], runs[run][1] - runs[run][0])
        return pltpu.make_async_remote_copy(
            src_ref=buf_out.at[part], dst_ref=buf_in.at[part], send_sem=xsend.at[sem], recv_sem=xrecv.at[sem],
            device_id={"replica": lax.rem(me + 1, replicas)}, device_id_type=MESH)

    for step in steps:
        for run in step:
            launch(q_send, q_recv, run, run, 1)
    q_recv[home] = q_send[home]
    forward(g_pro)
    begin(g_out)

    l_cache.wait()
    group = 8
    cols = group * cache.shape[1]
    row_id = lax.broadcasted_iota(jnp.int32, (group, cols), 0)
    col_id = lax.broadcasted_iota(jnp.int32, (group, cols), 1)
    position = (col_id - row_id * cache.shape[1]).astype(F32)
    def cached_part(g):
        part = slice(g * group, (g + 1) * group)
        q4 = jnp.concatenate([split_heads(q_rows[hp, part]) for hp in range(2)], axis=0)
        keys = cache[part].reshape(cols, 128)
        alive = (position >= 0) & (position < jnp.broadcast_to(len_col[part], (group, cols)))
        alive = jnp.concatenate((alive,) * 4, axis=0)
        scores = jnp.where(alive, dot_t(q4, keys), -jnp.inf)
        top = jnp.max(scores, axis=1, keepdims=True)
        weights = jnp.exp2(scores * base2 - top * base2).astype(BF)
        mixed = dot(weights, with_ones(keys))
        for hp in range(2):
            joined = join_heads(mixed[hp * 2 * group:(hp + 1) * 2 * group], top[hp * 2 * group:(hp + 1) * 2 * group])
            for i in range(3):
                past[i, hp, part] = joined[i]

    for g in range(12):
        cached_part(g)

    def attend(q, local=None):
        scores = dot_t(q, prefix[...])
        top = jnp.max(scores, axis=1, keepdims=True)
        if local is not None:
            near = dot_t(q, local)
            m = near.shape[1]
            seen = (lax.broadcasted_iota(jnp.int32, near.shape, 1)
                    <= lax.rem(lax.broadcasted_iota(jnp.int32, near.shape, 0), m))
            near = jnp.where(seen, near, -jnp.inf)
            top = jnp.maximum(top, jnp.max(near, axis=1, keepdims=True))
        shift = top * base2
        mixed = dot(jnp.exp2(scores * base2 - shift).astype(BF), ones_prefix[...])
        if local is not None:
            mixed = mixed + dot(jnp.exp2(near * base2 - shift).astype(BF), with_ones(local))
        return join_heads(mixed, top)

    l_pro.wait()
    arrived(g_pro)
    q_pro, kv_pro = project(0)
    for hp in range(2):
        above, total, _ = attend(split_heads(q_pro[:, hp * 128:(hp + 1) * 128].astype(F32)), kv_pro)
        att[0, x, :, hp * 128:(hp + 1) * 128] = (above / total).astype(BF)

    def share(base, s):
        own = att.at[s, x]
        return gather(base, (own.at[A], own.at[B]), att.at[s])

    a_pro = share(18, 0)
    begin(a_pro)

    lane = lax.rem(lax.broadcasted_iota(jnp.int32, (per * 8, 128), 1), HEAD)

    def serve(step):
        first = min(runs[run][0] for run in steps[step])
        for run in steps[step]:
            whole_run(q_send, q_recv, run, run).wait_recv()
        rows = q_recv[first:first + per].astype(F32).reshape(per * 8, 128)
        above, total, top = attend(split_heads(rows))
        level = top * scale + jnp.log(total)
        hi = level.astype(BF).astype(F32)
        mid_part = (level - hi).astype(BF).astype(F32)
        lo = level - hi - mid_part
        stat = jnp.where(lane < 16, hi, jnp.where(lane < 32, mid_part, lo))
        packed = jnp.concatenate(
            ((above / total).reshape(per, 8, 128), stat.reshape(per, 8, 128)), axis=1)
        r_send[first:first + per] = packed.astype(BF)
        for run in steps[step]:
            launch(r_send, r_recv, run, 5 + run, -1)

    def sibling(i, quarter):
        return pltpu.make_async_remote_copy(
            src_ref=w_part.at[quarter], dst_ref=w_part.at[quarter], send_sem=wsem.at[i], recv_sem=wrecv.at[i],
            device_id={"replica": me + 1 - 2 * core}, device_id_type=MESH)

    def settle(s):
        for d in range(4):
            cols = slice(d * width, (d + 1) * width)
            mixed = 0.0
            for g in range(4):
                mixed = mixed + dot(att[s, g], wo[g, :, cols]).astype(BF).astype(F32)
            mid[s, d] = (rows_in[s, d].astype(F32) + mixed).astype(BF)

    def hidden_of(s):
        normed = norm([mid[s, d] for d in range(4)], gain_m[...])
        gate = dot(normed, wg[...])
        up = dot(normed, wu[...])
        return (gate / (1.0 + jnp.exp(-gate)) * up).astype(BF)

    serve(0)
    serve(1)
    serve(2)
    serve(3)
    forward(g_out)
    r_recv[home] = r_send[home]
    for g in range(12, 16):
        cached_part(g)
    for step in steps:
        for run in step:
            whole_run(r_send, r_recv, run, 5 + run).wait_recv()
    back = dot(take[...], r_recv[...].reshape(2 * slots, 128))
    far_mix = back[:2 * n]
    e_row = lax.broadcasted_iota(jnp.int32, (128, 128), 0)
    e_col = lax.broadcasted_iota(jnp.int32, (128, 128), 1)
    pick = ((e_row < HEAD) == (e_col < HEAD)) & (
        (lax.rem(e_row, HEAD) == 0) | (lax.rem(e_row, HEAD) == 16) | (lax.rem(e_row, HEAD) == 32))
    far_level = dot(back[2 * n:].astype(BF), jnp.where(pick, 1.0, 0.0).astype(BF))
    q2 = q_rows[...].reshape(2 * n, 128)
    kv = kv_req.astype(F32)
    low = low_lanes(kv.shape)
    key2 = jnp.where(low, kv, swap(kv))
    val2 = jnp.where(low, swap(kv), kv)
    key2 = jnp.concatenate((key2, key2), axis=0)
    val2 = jnp.concatenate((val2, val2), axis=0)
    prod = q2 * key2
    low2 = low_lanes(prod.shape)
    own_even = jnp.sum(jnp.where(low2, prod, 0.0), axis=1, keepdims=True)
    own_odd = jnp.sum(jnp.where(low2, 0.0, prod), axis=1, keepdims=True)
    own = jnp.where(low2, jnp.broadcast_to(own_even, prod.shape), jnp.broadcast_to(own_odd, prod.shape)) * scale
    p_mix, p_total, p_top = past[0].reshape(2 * n, 128), past[1].reshape(2 * n, 128), past[2].reshape(2 * n, 128) * scale
    top = jnp.maximum(jnp.maximum(far_level, p_top), own)
    w_far, w_past, w_own = jnp.exp(far_level - top), jnp.exp(p_top - top), jnp.exp(own - top)
    merged = (far_mix * w_far + p_mix * w_past + val2 * w_own) / (w_far + p_total * w_past + w_own)
    att[1, x] = jnp.concatenate((merged[:n], merged[n:]), axis=1).astype(BF)

    a_req = share(24, 1)
    begin(a_req)
    forward(a_pro)
    siblings = [sibling(0, xl), sibling(1, xr), sibling(2, x2)]
    g_out[2].wait_recv()
    siblings[0].start()
    g_out[3].wait_recv()
    siblings[1].start()
    for c in l_wo:
        c.wait()
    l_gm.wait()
    l_wg.wait()
    l_wu.wait()
    for c in l_wd:
        c.wait()
    forward(a_req)
    g_out[4].wait_recv()
    g_out[5].wait_recv()
    siblings[2].start()
    arrived(a_req)
    for c in siblings:
        c.wait_recv()
    settle(1)
    hid_r = hidden_of(1)
    d_req = scatter(30, 1)
    spread(d_req, 1, lambda d: dot(hid_r, wd[d]))
    arrived(a_pro)
    settle(0)
    fold(d_req, 1)
    hid = hidden_of(0)
    d_pro = scatter(36, 0)
    spread(d_pro, 0, lambda d: dot(hid, wd[d]))
    fold(d_pro, 0)
    request_out[...] = (mid[1, x].astype(F32) + summed(d_req, 1)).astype(BF)
    prompt_out[...] = (mid[0, x].astype(F32) + summed(d_pro, 0)).astype(BF)

    for c in siblings:
        c.wait_send()
    for c in sent:
        c.wait_send()
    for run in runs:
        whole_run(q_send, q_recv, run, run).wait_send()
        whole_run(r_send, r_recv, run, 5 + run).wait_send()


def hand_over(a, b, c, d):
    c[...] = a[...]
    d[...] = b[...]


def body(
    prompt_rows, request_rows, request_keyval_cache, cache_len, destination, prefix_cache,
    attn_gain, w_query, keyval_weight, w_out, mlp_gain, w_gate, w_up, w_down,
):
    replicas = lax.axis_size("replica")
    n, width = request_rows.shape
    model = w_query.shape[0]
    units = w_gate.shape[1]
    cached = request_keyval_cache.shape[1]
    pre = prefix_cache.shape[0]
    V = pltpu.VMEM
    DMA = pltpu.SemaphoreType.DMA
    out = jax.ShapeDtypeStruct((n, width), BF)
    anyspec = pl.BlockSpec(memory_space=pl.ANY)
    vspec = pl.BlockSpec(memory_space=pltpu.VMEM)
    half = n // 2
    held = pl.pallas_call(
        functools.partial(kernel, replicas),
        out_shape=(out, out),
        in_specs=[anyspec] * 14,
        out_specs=(vspec, vspec),
        scratch_shapes=[
            V((1, n), jnp.int32), V((1, n), jnp.int32), V((1, model), F32), V((1, model), F32),
            V((2, 4, n, width), BF), V((2, 4, n, width), BF),
            V((pre, 128), BF), V((pre, 128), BF), V((n, cached, 128), BF),
            V((model, 256), BF), V((model, 128), BF), V((4, 2 * n, model), BF),
            V((model, units), BF), V((model, units), BF), V((4, units, width), BF),
            V((replicas * 8, 2 * n), BF), V((4 * n, replicas * 16), BF), V((2, n, 128), F32),
            V((replicas, 8, 128), BF), V((replicas, 8, 128), BF),
            V((replicas, 16, 128), BF), V((replicas, 16, 128), BF),
            V((3, 2, n, 128), F32), V((8, 128), BF),
            V((2, 4, n, width), BF), V((2, 2, half, width), BF),
            V((2, n, width), BF), V((2, n, width), BF), V((2, 2, half, width), BF), V((2, 4, n, 256), BF), DMA((3,)), DMA((3,)),
            DMA((20,)), DMA((42,)), DMA((42,)), DMA((10,)), DMA((10,)),
        ],
        compiler_params=pltpu.CompilerParams(
            collective_id=0, has_side_effects=True, vmem_limit_bytes=60 * 1024 * 1024),
    )(
        prompt_rows, request_rows, request_keyval_cache, cache_len.reshape(1, n), destination.reshape(1, n), prefix_cache,
        attn_gain.reshape(1, model), w_query, keyval_weight, w_out, mlp_gain.reshape(1, model), w_gate, w_up, w_down,
    )
    return pl.pallas_call(
        hand_over, out_shape=(out, out), in_specs=[vspec, vspec], out_specs=(vspec, vspec))(*held)


def solution(mesh):
    return jax.shard_map(
        body,
        mesh=mesh,
        in_specs=(
            P("replica", "tensor"), P("replica", "tensor"), P("replica", None, "tensor"), P("replica"),
            P("replica", None), P("replica", "tensor"), P(), P(None, "tensor"), P(None, "tensor"),
            P("tensor", None), P(), P(None, "tensor"), P(None, "tensor"), P("tensor", None),
        ),
        out_specs=(P("replica", "tensor"), P("replica", "tensor")),
        check_vma=False,
    )
```

```python
import functools
import math

import jax
import jax.numpy as jnp
from jax import lax
from jax.experimental import pallas as pl
from jax.experimental.pallas import tpu as pltpu
from jax.sharding import PartitionSpec as P

HEAD = 64
EPS = 1e-05
BF = jnp.bfloat16
F32 = jnp.float32
MESH = pl.DeviceIdType.MESH
LOG2E = math.log2(math.e)


def dot(a, b):
    return jnp.dot(a, b, preferred_element_type=F32)


def dot_t(a, b):
    return lax.dot_general(a, b, (((1,), (1,)), ((), ())), preferred_element_type=F32)


def low_lanes(shape):
    return lax.broadcasted_iota(jnp.int32, shape, len(shape) - 1) % 128 < HEAD


def swap(v):
    return pltpu.roll(v, HEAD, 1)


def split_heads(v):
    low = low_lanes(v.shape)
    return jnp.concatenate((jnp.where(low, v, 0.0), jnp.where(low, swap(v), 0.0)), axis=0).astype(BF)


def join_heads(mixed, top):
    n = mixed.shape[0] // 2
    even, odd = mixed[:n], mixed[n:]
    low = low_lanes(even.shape)
    return (
        jnp.where(low, swap(even), odd),
        jnp.where(low, even, swap(odd)),
        jnp.where(low, jnp.broadcast_to(top[:n], even.shape), jnp.broadcast_to(top[n:], even.shape)),
    )


def with_ones(keyval):
    return jnp.where(low_lanes(keyval.shape), jnp.ones_like(keyval), keyval)


def norm(pieces, gain):
    values = jnp.concatenate([p.astype(F32) for p in pieces], axis=1)
    inv_scale = lax.rsqrt(jnp.mean(values * values, axis=1, keepdims=True) + EPS)
    return (values * inv_scale * gain).astype(BF)


def kernel(
    replicas,
    prompt_hbm, request_hbm, cache_hbm, len_hbm, dest_hbm, prefix_hbm, gain_a_hbm, wq_hbm, wkv_hbm, wo_hbm,
    gain_m_hbm, wg_hbm, wu_hbm, wd_hbm,
    prompt_out, request_out,
    dest_v, len_v, gain_a, gain_m, rows_in, mid, prefix, ones_prefix, cache, wq, wkv, wo, wg, wu, wd,
    put, take, q_rows, q_send, q_recv, r_send, r_recv, past, res, terms, far2, from_l, from_r, folded, att, wsem, wrecv,
    lsem, ssem, rsem, xsend, xrecv,
):
    half, width = rows_in.shape[2] // 2, rows_in.shape[3]
    x = lax.axis_index("tensor")
    me = lax.axis_index("replica")
    xr, xl, x2 = lax.rem(x + 1, 4), lax.rem(x + 3, 4), lax.rem(x + 2, 4)
    right, left = {"tensor": xr}, {"tensor": xl}
    scale = HEAD ** -0.5
    base2 = scale * LOG2E
    A, B = pl.ds(0, half), pl.ds(half, half)

    barrier = pltpu.get_barrier_semaphore()
    pl.semaphore_signal(barrier, inc=1, device_id=right, device_id_type=MESH)
    pl.semaphore_signal(barrier, inc=1, device_id=left, device_id_type=MESH)

    def greet(k, c):
        pl.semaphore_signal(barrier, inc=1, device_id={"replica": lax.rem(me + k, replicas)}, device_id_type=MESH)
        return c

    lax.fori_loop(1, replicas, greet, 0)

    loads = []

    def load(src, dst):
        copy = pltpu.make_async_copy(src, dst, lsem.at[len(loads)])
        copy.start()
        loads.append(copy)
        return copy

    l_dest, l_len = load(dest_hbm, dest_v), load(len_hbm, len_v)
    l_ga, l_gm = load(gain_a_hbm, gain_a), load(gain_m_hbm, gain_m)
    l_req, l_pro = load(request_hbm, rows_in.at[1, x]), load(prompt_hbm, rows_in.at[0, x])
    l_wq, l_wkv = load(wq_hbm, wq), load(wkv_hbm, wkv)
    l_prefix, l_cache = load(prefix_hbm, prefix), load(cache_hbm, cache)
    part_rows = wo.shape[1] // 2
    l_wo = [load(wo_hbm, wo.at[x])]
    l_wg, l_wu = load(wg_hbm, wg), load(wu_hbm, wu)
    l_wd = [load(wd_hbm.at[:, pl.ds(d * width, width)], wd.at[d]) for d in range(4)]

    pl.semaphore_wait(barrier, replicas + 1)

    sent = []

    def ring(base, i, src, dst, to):
        copy = pltpu.make_async_remote_copy(
            src_ref=src, dst_ref=dst, send_sem=ssem.at[base + i], recv_sem=rsem.at[base + i],
            device_id=to, device_id_type=MESH)
        sent.append(copy)
        return copy

    def gather(base, own, whole, A=A, B=B):
        own_a, own_b = own
        return [
            ring(base, 0, own_a, whole.at[x, A], right), ring(base, 1, own_b, whole.at[x, B], left),
            ring(base, 2, own_b, whole.at[x, B], right), ring(base, 3, own_a, whole.at[x, A], left),
            ring(base, 4, whole.at[xl, A], whole.at[xl, A], right), ring(base, 5, whole.at[xr, B], whole.at[xr, B], left),
        ]

    def begin(msgs):
        for m in msgs[:4]:
            m.start()

    def forward(msgs):
        for i in range(2):
            msgs[i].wait_recv()
            msgs[4 + i].start()

    def arrived(msgs):
        for m in msgs[2:]:
            m.wait_recv()

    def scatter(base, s):
        t = terms.at[s]
        return [
            ring(base, 0, t.at[x2, A], far2.at[s, 0], right), ring(base, 1, t.at[x2, B], far2.at[s, 1], left),
            ring(base, 2, t.at[xr, B], from_l.at[s, B], right), ring(base, 3, t.at[xl, A], from_r.at[s, A], left),
            ring(base, 4, folded.at[s, 0], from_l.at[s, A], right), ring(base, 5, folded.at[s, 1], from_r.at[s, B], left),
        ]

    def spread(msgs, s, make):
        terms[s, x2] = make(x2).astype(BF)
        msgs[0].start()
        msgs[1].start()
        terms[s, xr] = make(xr).astype(BF)
        msgs[2].start()
        terms[s, xl] = make(xl).astype(BF)
        msgs[3].start()
        terms[s, x] = make(x).astype(BF)

    def fold(msgs, s):
        for i, part in enumerate(((xr, A), (xl, B))):
            msgs[i].wait_recv()
            folded[s, i] = (terms[s, part[0], part[1]].astype(F32) + far2[s, i].astype(F32)).astype(BF)
            msgs[4 + i].start()

    def summed(msgs, s):
        for m in msgs[2:]:
            m.wait_recv()
        return terms[s, x].astype(F32) + (from_l[s].astype(F32) + from_r[s].astype(F32))

    g_req = gather(0, (request_hbm.at[A], request_hbm.at[B]), rows_in.at[1])
    g_pro = gather(6, (prompt_hbm.at[A], prompt_hbm.at[B]), rows_in.at[0])
    core = lax.rem(me, 2)
    odd = lax.rem(me // 2, 2)
    share_rows = part_rows // 4
    w_base = pl.multiple_of(core * part_rows, part_rows)
    w_part = wo.at[:, pl.ds(w_base, part_rows)]
    w_mine = pl.multiple_of(w_base + odd * share_rows, share_rows)
    w_own = wo.at[:, pl.ds(w_mine, share_rows)]
    q = share_rows // 2
    g_own = gather(
        12, (wo_hbm.at[pl.ds(w_mine, q)], wo_hbm.at[pl.ds(w_mine + q, q)]), w_own, pl.ds(0, q), pl.ds(q, q))
    w_rest = pl.multiple_of(w_base + 2 * share_rows, share_rows)
    g_out = gather(
        42, (wo_hbm.at[pl.ds(w_rest, share_rows)], wo_hbm.at[pl.ds(w_rest + share_rows, share_rows)]),
        wo.at[:, pl.ds(w_rest, 2 * share_rows)], pl.ds(0, share_rows), pl.ds(share_rows, share_rows))

    def across(i, quarter):
        return pltpu.make_async_remote_copy(
            src_ref=w_own.at[quarter], dst_ref=w_own.at[quarter], send_sem=wsem.at[3 + i], recv_sem=wrecv.at[3 + i],
            device_id={"replica": me + 2 - 4 * odd}, device_id_type=MESH)

    acrosses = [across(0, xl), across(1, xr), across(2, x2)]
    begin(g_req)

    n = dest_v.shape[1]
    l_dest.wait()
    eye = lax.broadcasted_iota(jnp.int32, (n, n), 0) - lax.broadcasted_iota(jnp.int32, (n, n), 1)
    dest_row = dest_v[...].astype(F32)
    dest_mat = jnp.broadcast_to(dest_row, (n, n))
    dest_col = jnp.sum(jnp.where(eye == 0, dest_mat, 0.0), axis=1, keepdims=True)
    same = dest_mat == jnp.broadcast_to(dest_col, (n, n))
    rank_col = jnp.sum(jnp.where(same & (eye > 0), 1.0, 0.0), axis=1, keepdims=True)
    rank_row = jnp.sum(jnp.where(same & (eye < 0), 1.0, 0.0), axis=0, keepdims=True)
    me_f = me.astype(F32)
    turn = replicas * 3 // 8
    home = replicas - turn

    def block_of(dest):
        gap = dest - me_f - turn
        gap = jnp.where(gap < 0, gap + replicas, gap)
        return jnp.where(gap < 0, gap + replicas, gap)

    put_row = block_of(dest_row) * 8 + rank_row
    put_row = jnp.concatenate((put_row, put_row + 4), axis=1)
    slots = replicas * 8
    put[...] = jnp.where(
        jnp.broadcast_to(put_row, (slots, 2 * n)) == lax.broadcasted_iota(jnp.int32, (slots, 2 * n), 0).astype(F32),
        1.0, 0.0).astype(BF)
    take_col = block_of(dest_col) * 16 + rank_col
    take_col = jnp.concatenate((take_col, take_col + 4, take_col + 8, take_col + 12), axis=0)
    take[...] = jnp.where(
        jnp.broadcast_to(take_col, (4 * n, 2 * slots))
        == lax.broadcasted_iota(jnp.int32, (4 * n, 2 * slots), 1).astype(F32), 1.0, 0.0).astype(BF)

    l_prefix.wait()
    ones_prefix[...] = with_ones(prefix[...])
    l_len.wait()
    len_mat = jnp.broadcast_to(len_v[...].astype(F32), (n, n))
    len_col = jnp.sum(jnp.where(eye == 0, len_mat, 0.0), axis=1, keepdims=True)

    forward(g_req)
    begin(g_pro)
    l_ga.wait()
    l_wq.wait()
    l_wkv.wait()
    l_req.wait()
    arrived(g_req)

    def project(s):
        normed = norm([rows_in[s, d] for d in range(4)], gain_a[...])
        return dot(normed, wq[...]).astype(BF), dot(normed, wkv[...]).astype(BF)

    q_req, kv_req = project(1)
    stacked = jnp.concatenate((q_req[:, :128], q_req[:, 128:]), axis=0)
    q_rows[0] = stacked[:n].astype(F32)
    q_rows[1] = stacked[n:].astype(F32)
    q_send[...] = dot(put[...], stacked).reshape(replicas, 8, 128).astype(BF)

    per = replicas // 4
    runs = {0: (0, per), 1: (per, 2 * per), 2: (2 * per, home), 3: (3 * per, 4 * per), 4: (home + 1, 3 * per)}
    steps = ((0,), (1,), (3,), (2, 4))

    def travel(buf_out, buf_in, kk, sem, sign):
        return pltpu.make_async_remote_copy(
            src_ref=buf_out.at[kk], dst_ref=buf_in.at[kk], send_sem=xsend.at[sem], recv_sem=xrecv.at[sem],
            device_id={"replica": lax.rem(me + 2 * replicas + sign * (kk + turn), replicas)}, device_id_type=MESH)

    def launch(buf_out, buf_in, run, sem, sign):
        def one(kk, c):
            travel(buf_out, buf_in, kk, sem, sign).start()
            return c
        lax.fori_loop(runs[run][0], runs[run][1], one, 0)

    def whole_run(buf_out, buf_in, run, sem):
        part = pl.ds(runs[run][0], runs[run][1] - runs[run][0])
        return pltpu.make_async_remote_copy(
            src_ref=buf_out.at[part], dst_ref=buf_in.at[part], send_sem=xsend.at[sem], recv_sem=xrecv.at[sem],
            device_id={"replica": lax.rem(me + 1, replicas)}, device_id_type=MESH)

    for step in steps:
        for run in step:
            launch(q_send, q_recv, run, run, 1)
    q_recv[home] = q_send[home]
    forward(g_pro)
    begin(g_own)

    l_cache.wait()
    group = 8
    cols = group * cache.shape[1]
    row_id = lax.broadcasted_iota(jnp.int32, (group, cols), 0)
    col_id = lax.broadcasted_iota(jnp.int32, (group, cols), 1)
    position = (col_id - row_id * cache.shape[1]).astype(F32)
    def cached_part(g):
        part = slice(g * group, (g + 1) * group)
        q4 = jnp.concatenate([split_heads(q_rows[hp, part]) for hp in range(2)], axis=0)
        keys = cache[part].reshape(cols, 128)
        alive = (position >= 0) & (position < jnp.broadcast_to(len_col[part], (group, cols)))
        alive = jnp.concatenate((alive,) * 4, axis=0)
        scores = jnp.where(alive, dot_t(q4, keys), -jnp.inf)
        top = jnp.max(scores, axis=1, keepdims=True)
        weights = jnp.exp2(scores * base2 - top * base2).astype(BF)
        mixed = dot(weights, with_ones(keys))
        for hp in range(2):
            joined = join_heads(mixed[hp * 2 * group:(hp + 1) * 2 * group], top[hp * 2 * group:(hp + 1) * 2 * group])
            for i in range(3):
                past[i, hp, part] = joined[i]

    for g in range(12):
        cached_part(g)

    def attend(q, local=None):
        scores = dot_t(q, prefix[...])
        top = jnp.max(scores, axis=1, keepdims=True)
        if local is not None:
            near = dot_t(q, local)
            m = near.shape[1]
            seen = (lax.broadcasted_iota(jnp.int32, near.shape, 1)
                    <= lax.rem(lax.broadcasted_iota(jnp.int32, near.shape, 0), m))
            near = jnp.where(seen, near, -jnp.inf)
            top = jnp.maximum(top, jnp.max(near, axis=1, keepdims=True))
        shift = top * base2
        mixed = dot(jnp.exp2(scores * base2 - shift).astype(BF), ones_prefix[...])
        if local is not None:
            mixed = mixed + dot(jnp.exp2(near * base2 - shift).astype(BF), with_ones(local))
        return join_heads(mixed, top)

    l_pro.wait()
    arrived(g_pro)
    q_pro, kv_pro = project(0)
    for hp in range(2):
        above, total, _ = attend(split_heads(q_pro[:, hp * 128:(hp + 1) * 128].astype(F32)), kv_pro)
        att[0, x, :, hp * 128:(hp + 1) * 128] = (above / total).astype(BF)

    def share(base, s):
        own = att.at[s, x]
        return gather(base, (own.at[A], own.at[B]), att.at[s])

    a_pro = share(18, 0)
    forward(g_own)
    begin(g_out)
    begin(a_pro)

    lane = lax.rem(lax.broadcasted_iota(jnp.int32, (per * 8, 128), 1), HEAD)

    def serve(step):
        first = min(runs[run][0] for run in steps[step])
        for run in steps[step]:
            whole_run(q_send, q_recv, run, run).wait_recv()
        rows = q_recv[first:first + per].astype(F32).reshape(per * 8, 128)
        above, total, top = attend(split_heads(rows))
        level = top * scale + jnp.log(total)
        hi = level.astype(BF).astype(F32)
        mid_part = (level - hi).astype(BF).astype(F32)
        lo = level - hi - mid_part
        stat = jnp.where(lane < 16, hi, jnp.where(lane < 32, mid_part, lo))
        packed = jnp.concatenate(
            ((above / total).reshape(per, 8, 128), stat.reshape(per, 8, 128)), axis=1)
        r_send[first:first + per] = packed.astype(BF)
        for run in steps[step]:
            launch(r_send, r_recv, run, 5 + run, -1)

    def sibling(i, quarter):
        return pltpu.make_async_remote_copy(
            src_ref=w_part.at[quarter], dst_ref=w_part.at[quarter], send_sem=wsem.at[i], recv_sem=wrecv.at[i],
            device_id={"replica": me + 1 - 2 * core}, device_id_type=MESH)

    def settle(s):
        for d in range(4):
            cols = slice(d * width, (d + 1) * width)
            mixed = 0.0
            for g in range(4):
                mixed = mixed + dot(att[s, g], wo[g, :, cols]).astype(BF).astype(F32)
            mid[s, d] = (rows_in[s, d].astype(F32) + mixed).astype(BF)

    def hidden_of(s):
        normed = norm([mid[s, d] for d in range(4)], gain_m[...])
        gate = dot(normed, wg[...])
        up = dot(normed, wu[...])
        return (gate / (1.0 + jnp.exp(-gate)) * up).astype(BF)

    serve(0)
    for i in range(2):
        g_own[2 + i].wait_recv()
        acrosses[i].start()
    serve(1)
    serve(2)
    g_own[4].wait_recv()
    g_own[5].wait_recv()
    acrosses[2].start()
    serve(3)
    forward(g_out)
    r_recv[home] = r_send[home]
    for g in range(12, 16):
        cached_part(g)
    for step in steps:
        for run in step:
            whole_run(r_send, r_recv, run, 5 + run).wait_recv()
    back = dot(take[...], r_recv[...].reshape(2 * slots, 128))
    far_mix = back[:2 * n]
    e_row = lax.broadcasted_iota(jnp.int32, (128, 128), 0)
    e_col = lax.broadcasted_iota(jnp.int32, (128, 128), 1)
    pick = ((e_row < HEAD) == (e_col < HEAD)) & (
        (lax.rem(e_row, HEAD) == 0) | (lax.rem(e_row, HEAD) == 16) | (lax.rem(e_row, HEAD) == 32))
    far_level = dot(back[2 * n:].astype(BF), jnp.where(pick, 1.0, 0.0).astype(BF))
    q2 = q_rows[...].reshape(2 * n, 128)
    kv = kv_req.astype(F32)
    low = low_lanes(kv.shape)
    key2 = jnp.where(low, kv, swap(kv))
    val2 = jnp.where(low, swap(kv), kv)
    key2 = jnp.concatenate((key2, key2), axis=0)
    val2 = jnp.concatenate((val2, val2), axis=0)
    prod = q2 * key2
    low2 = low_lanes(prod.shape)
    own_even = jnp.sum(jnp.where(low2, prod, 0.0), axis=1, keepdims=True)
    own_odd = jnp.sum(jnp.where(low2, 0.0, prod), axis=1, keepdims=True)
    own = jnp.where(low2, jnp.broadcast_to(own_even, prod.shape), jnp.broadcast_to(own_odd, prod.shape)) * scale
    p_mix, p_total, p_top = past[0].reshape(2 * n, 128), past[1].reshape(2 * n, 128), past[2].reshape(2 * n, 128) * scale
    top = jnp.maximum(jnp.maximum(far_level, p_top), own)
    w_far, w_past, w_own = jnp.exp(far_level - top), jnp.exp(p_top - top), jnp.exp(own - top)
    merged = (far_mix * w_far + p_mix * w_past + val2 * w_own) / (w_far + p_total * w_past + w_own)
    att[1, x] = jnp.concatenate((merged[:n], merged[n:]), axis=1).astype(BF)

    a_req = share(24, 1)
    begin(a_req)
    forward(a_pro)
    siblings = [sibling(0, xl), sibling(1, xr), sibling(2, x2)]
    for i in range(2):
        acrosses[i].wait_recv()
        g_out[2 + i].wait_recv()
        siblings[i].start()
    for c in l_wo:
        c.wait()
    l_gm.wait()
    l_wg.wait()
    l_wu.wait()
    for c in l_wd:
        c.wait()
    acrosses[2].wait_recv()
    g_out[4].wait_recv()
    g_out[5].wait_recv()
    siblings[2].start()
    forward(a_req)
    arrived(a_pro)
    for c in siblings:
        c.wait_recv()
    settle(0)
    hid = hidden_of(0)
    d_pro = scatter(36, 0)
    spread(d_pro, 0, lambda d: dot(hid, wd[d]))
    arrived(a_req)
    settle(1)
    fold(d_pro, 0)
    hid_r = hidden_of(1)
    d_req = scatter(30, 1)
    spread(d_req, 1, lambda d: dot(hid_r, wd[d]))
    prompt_out[...] = (mid[0, x].astype(F32) + summed(d_pro, 0)).astype(BF)
    fold(d_req, 1)
    request_out[...] = (mid[1, x].astype(F32) + summed(d_req, 1)).astype(BF)

    for c in acrosses:
        c.wait_send()
    for c in siblings:
        c.wait_send()
    for c in sent:
        c.wait_send()
    for run in runs:
        whole_run(q_send, q_recv, run, run).wait_send()
        whole_run(r_send, r_recv, run, 5 + run).wait_send()


def hand_over(a, b, c, d):
    c[...] = a[...]
    d[...] = b[...]


def body(
    prompt_rows, request_rows, request_keyval_cache, cache_len, destination, prefix_cache,
    attn_gain, w_query, keyval_weight, w_out, mlp_gain, w_gate, w_up, w_down,
):
    replicas = lax.axis_size("replica")
    n, width = request_rows.shape
    model = w_query.shape[0]
    units = w_gate.shape[1]
    cached = request_keyval_cache.shape[1]
    pre = prefix_cache.shape[0]
    V = pltpu.VMEM
    DMA = pltpu.SemaphoreType.DMA
    out = jax.ShapeDtypeStruct((n, width), BF)
    anyspec = pl.BlockSpec(memory_space=pl.ANY)
    vspec = pl.BlockSpec(memory_space=pltpu.VMEM)
    half = n // 2
    held = pl.pallas_call(
        functools.partial(kernel, replicas),
        out_shape=(out, out),
        in_specs=[anyspec] * 14,
        out_specs=(vspec, vspec),
        scratch_shapes=[
            V((1, n), jnp.int32), V((1, n), jnp.int32), V((1, model), F32), V((1, model), F32),
            V((2, 4, n, width), BF), V((2, 4, n, width), BF),
            V((pre, 128), BF), V((pre, 128), BF), V((n, cached, 128), BF),
            V((model, 256), BF), V((model, 128), BF), V((4, 2 * n, model), BF),
            V((model, units), BF), V((model, units), BF), V((4, units, width), BF),
            V((replicas * 8, 2 * n), BF), V((4 * n, replicas * 16), BF), V((2, n, 128), F32),
            V((replicas, 8, 128), BF), V((replicas, 8, 128), BF),
            V((replicas, 16, 128), BF), V((replicas, 16, 128), BF),
            V((3, 2, n, 128), F32), V((8, 128), BF),
            V((2, 4, n, width), BF), V((2, 2, half, width), BF),
            V((2, n, width), BF), V((2, n, width), BF), V((2, 2, half, width), BF), V((2, 4, n, 256), BF), DMA((6,)), DMA((6,)),
            DMA((20,)), DMA((48,)), DMA((48,)), DMA((10,)), DMA((10,)),
        ],
        compiler_params=pltpu.CompilerParams(
            collective_id=0, has_side_effects=True, vmem_limit_bytes=60 * 1024 * 1024),
    )(
        prompt_rows, request_rows, request_keyval_cache, cache_len.reshape(1, n), destination.reshape(1, n), prefix_cache,
        attn_gain.reshape(1, model), w_query, keyval_weight, w_out, mlp_gain.reshape(1, model), w_gate, w_up, w_down,
    )
    return pl.pallas_call(
        hand_over, out_shape=(out, out), in_specs=[vspec, vspec], out_specs=(vspec, vspec))(*held)


def solution(mesh):
    return jax.shard_map(
        body,
        mesh=mesh,
        in_specs=(
            P("replica", "tensor"), P("replica", "tensor"), P("replica", None, "tensor"), P("replica"),
            P("replica", None), P("replica", "tensor"), P(), P(None, "tensor"), P(None, "tensor"),
            P("tensor", None), P(), P(None, "tensor"), P(None, "tensor"), P("tensor", None),
        ),
        out_specs=(P("replica", "tensor"), P("replica", "tensor")),
        check_vma=False,
    )
```
